32 devices in a mesh: dp: 8 (over y, x, core), tensor: 4 (over z).
Axes of the slice: x: 2, y: 2, z: 4, core: 2. Of those that a mesh axis runs over, the one named last changes fastest.
Arguments:
- inputs_short: bfloat16 [16, 512, 1024], P('dp', 'tensor'), may hold values from -6 to 6
- memory_short: bfloat16 [16, 512, 1024], P('dp', 'tensor'), may hold values from -6 to 6
- compressed_short: bfloat16 [16, 512, 1024], P('dp', 'tensor'), may hold values from -6 to 6
- offsets_short: int32 [16], P('dp'), may hold values from 0 to 1024, as said below
- inputs_long: bfloat16 [8, 1024, 1024], P('dp', 'tensor'), may hold values from -6 to 6
- memory_long: bfloat16 [8, 1024, 1024], P('dp', 'tensor'), may hold values from -6 to 6
- compressed_long: bfloat16 [8, 1024, 1024], P('dp', 'tensor'), may hold values from -6 to 6
- offsets_long: int32 [8], P('dp'), may hold values from 0 to 2048, as said below
- query_weight: bfloat16 [1024, 1024], P(None, 'tensor'), may hold values from -0.1875 to 0.1875
- key_weight: bfloat16 [1024, 1024], P(None, 'tensor'), may hold values from -0.1875 to 0.1875
- value_weight: bfloat16 [1024, 1024], P(None, 'tensor'), may hold values from -0.1875 to 0.1875
- out_weight: bfloat16 [1024, 1024], P('tensor'), may hold values from -4 to 4
- up_weight: bfloat16 [1024, 4096], P(None, 'tensor'), may hold values from -0.1875 to 0.1875
- down_weight: bfloat16 [4096, 1024], P('tensor'), may hold values from -0.09375 to 0.09375
- compress_weight: bfloat16 [3, 1024, 1024], P(None, None, 'tensor'), may hold values from -0.109375 to 0.109375
- attention_gain: float32 [1024], replicated, may hold values from 0.5 to 1.5
- feedforward_gain: float32 [1024], replicated, may hold values from 0.5 to 1.5
- cotangent_short: bfloat16 [16, 512, 1024], P('dp', 'tensor'), may hold values from -6 to 6
- cotangent_long: bfloat16 [8, 1024, 1024], P('dp', 'tensor'), may hold values from -6 to 6
Outputs:
- output_short: bfloat16 [16, 512, 1024], P('dp', 'tensor')
- output_long: bfloat16 [8, 1024, 1024], P('dp', 'tensor')
- grad_inputs_short: float32 [16, 512, 1024], P('dp', 'tensor')
- grad_inputs_long: float32 [8, 1024, 1024], P('dp', 'tensor')
- appended_short: bfloat16 [16, 170, 1024], P('dp', None, 'tensor')
- appended_long: bfloat16 [8, 341, 1024], P('dp', None, 'tensor')
- grad_query_weight: float32 [1024, 1024], P(None, 'tensor')
- grad_key_weight: float32 [1024, 1024], P(None, 'tensor')
- grad_value_weight: float32 [1024, 1024], P(None, 'tensor')
- grad_out_weight: float32 [1024, 1024], P('tensor')
- grad_up_weight: float32 [1024, 4096], P(None, 'tensor')
- grad_down_weight: float32 [4096, 1024], P('tensor')
- grad_compress_weight: float32 [3, 1024, 1024], P(None, None, 'tensor')
- grad_attention_gain: float32 [1024], replicated
- grad_feedforward_gain: float32 [1024], replicated
- rebuild_loss: float32 [], replicated
The draws below stay inside these ranges and needn't reach their ends.
Inputs may be any that keep to these rules, and one draw needn't show every extreme that they name: `offsets_short`: number of leading rows without data in a short sequence; some sequence has none and some has all 1024. `offsets_long`: number of leading rows without data in a long sequence; some sequence has none and some has all 2048.
All inputs are finite; a program needn't handle non-finite values.
Results may differ from the reference program's by a relative error of at most 0.02.
Values may be sent and summed in bfloat16 or wider, within the bound.
A program may use at most 256 MiB of HBM per device.

```python
from functools import partial
import jax
import jax.numpy as jnp
from jax import lax

D = 1024
HEADS = 8
HEAD_SIZE = 128
FF = 4096
SHORT_LEN = 512
LONG_LEN = 1024
SHORT = 16
LONG = 8
ROWS_ALL = 16384


def draw_offsets_short(key, part):
    values = jax.random.randint(key, (SHORT,), 0, 2 * SHORT_LEN + 1)
    values = values.at[0].set(0).at[1].set(2 * SHORT_LEN)
    return values.astype(jnp.int32)


def draw_offsets_long(key, part):
    values = jax.random.randint(key, (LONG,), 0, 2 * LONG_LEN + 1)
    values = values.at[0].set(0).at[1].set(2 * LONG_LEN)
    return values.astype(jnp.int32)


def block_scale(own_key, extent, split, smallest, high):
    def one(position, shards_of):
        heights = jax.random.uniform(jax.random.fold_in(jax.random.fold_in(own_key, 6), position), (shards_of,), jnp.float32, smallest / len(split), high / len(split))
        return jnp.repeat(jnp.exp(heights), extent[position] // shards_of).reshape((-1,) + (1,) * (len(extent) - position - 1))

    loudness = one(*split[0])
    for cut in split[1:]:
        loudness = loudness * one(*cut)
    return loudness


def noise(stream_key, dims, deviation, bound, pieces=(), kind=jnp.bfloat16):
    entries = jax.random.normal(stream_key, dims, jnp.float32) * deviation
    if len(pieces) > 0:
        entries = block_scale(stream_key, dims, pieces, -0.22, 0.18) * entries
    return jnp.clip(entries, min=-bound, max=bound).astype(kind)


def setup_inputs(seed: int = 0) -> dict:
    key_of = jax.random.split(jax.random.key(seed), 20)
    inputs_short = noise(key_of[0], (SHORT, SHORT_LEN, D), 1.0, 6.0, ((0, 8), (1, 4)))
    memory_short = noise(key_of[1], (SHORT, SHORT_LEN, D), 1.0, 6.0, ((0, 8), (1, 4)))
    compressed_short = noise(key_of[2], (SHORT, SHORT_LEN, D), 1.0, 6.0, ((0, 8), (1, 4)))
    offsets_short = draw_offsets_short(jax.random.fold_in(key_of[19], 71), 0)
    inputs_long = noise(key_of[4], (LONG, LONG_LEN, D), 1.0, 6.0, ((0, 8), (1, 4)))
    memory_long = noise(key_of[5], (LONG, LONG_LEN, D), 1.0, 6.0, ((0, 8), (1, 4)))
    compressed_long = noise(key_of[6], (LONG, LONG_LEN, D), 1.0, 6.0, ((0, 8), (1, 4)))
    offsets_long = draw_offsets_long(jax.random.fold_in(key_of[19], 71), 0)
    query_weight = noise(key_of[8], (D, D), D ** -0.5, 0.1875, ((1, 4),))
    key_weight = noise(key_of[9], (D, D), D ** -0.5, 0.1875, ((1, 4),))
    value_weight = noise(key_of[10], (D, D), D ** -0.5, 0.1875, ((1, 4),))
    out_weight = noise(key_of[11], (D, D), (D // SHORT_LEN) ** -0.5, 4.0, ((0, 4),))
    up_weight = noise(key_of[12], (D, FF), D ** -0.5, 0.1875, ((1, 4),))
    down_weight = noise(key_of[13], (FF, D), FF ** -0.5, 0.09375, ((0, 4),))
    compress_weight = noise(key_of[14], (3, D, D), (3 * D) ** -0.5, 0.109375, ((2, 4),))
    attention_gain = jnp.clip(1.0 + 0.1 * jax.random.normal(key_of[15], (D,), jnp.float32), 0.5, 1.5)
    feedforward_gain = jnp.clip(1.0 + 0.1 * jax.random.normal(key_of[16], (D,), jnp.float32), 0.5, 1.5)
    cotangent_short = noise(key_of[17], (SHORT, SHORT_LEN, D), 1.0, 6.0, ((0, 8), (1, 4)))
    cotangent_long = noise(key_of[18], (LONG, LONG_LEN, D), 1.0, 6.0, ((0, 8), (1, 4)))
    return dict(inputs_short=inputs_short, memory_short=memory_short, compressed_short=compressed_short, offsets_short=offsets_short, inputs_long=inputs_long, memory_long=memory_long, compressed_long=compressed_long, offsets_long=offsets_long, query_weight=query_weight, key_weight=key_weight, value_weight=value_weight, out_weight=out_weight, up_weight=up_weight, down_weight=down_weight, compress_weight=compress_weight, attention_gain=attention_gain, feedforward_gain=feedforward_gain, cotangent_short=cotangent_short, cotangent_long=cotangent_long)


epsilon = 1e-05
rebuild_weight = 256.0
masked_value = -1e+30
highest = lax.Precision.HIGHEST

@jax.custom_vjp
def low(v):
    return lax.optimization_barrier(v.astype(jnp.bfloat16)).astype(jnp.float32)

@jax.custom_vjp
def low_back(v):
    return v

def low_keep(v):
    return (low(v), None)

def low_pass(kept, grad):
    return (grad,)

def back_keep(v):
    return (v, None)

def back_low(kept, grad):
    return (low(grad),)
low.defvjp(low_keep, low_pass)
low_back.defvjp(back_keep, back_low)

def product(left, right):
    return jnp.dot(left, right, precision=highest)

def layer_norm(rows, gain):
    mean = lax.optimization_barrier(jnp.mean(rows, -1, keepdims=True))
    centred = rows - mean
    return centred * lax.rsqrt(lax.optimization_barrier(jnp.mean(centred * centred, -1, keepdims=True)) + epsilon) * gain

def to_heads(array):
    return array.reshape(array.shape[0], HEADS, HEAD_SIZE)

def attend(query, key, value, validity):
    scores = low_back(jnp.einsum('qhd,khd->hqk', query, key, precision=highest) * HEAD_SIZE ** (-0.5))
    if validity is not None:
        scores = jnp.where(validity[None], scores, masked_value)
    weights = low(jax.nn.softmax(scores, -1))
    return low_back(jnp.einsum('hqk,khd->qhd', weights, value, precision=highest))

def sequence_pass(params, fixed, item):
    query_projection_weight, key_w, value_w, output_projection_weight, up_projection_weight, down_projection_weight, squeeze_w, attention_gain, feedforward_gain = params
    fixed_query, fixed_key, fixed_value, fixed_gain = fixed
    inputs, memory, older, offset, fixed_inputs = item
    length = inputs.shape[0]
    normed = low(layer_norm(inputs, attention_gain))
    memory_rows = low(layer_norm(jnp.concatenate([older, memory], 0), attention_gain))
    incoming_keys = jnp.concatenate([memory_rows, normed], 0)
    queries = to_heads(low_back(low(product(normed, query_projection_weight))))
    keys = to_heads(low_back(low(product(incoming_keys, key_w))))
    values = to_heads(low_back(low(product(incoming_keys, value_w))))
    query_place = jnp.arange(length)[:, None]
    key_place = jnp.arange(3 * length)[None, :]
    validity = jnp.where(key_place < 2 * length, key_place >= offset, key_place - 2 * length <= query_place)
    attention = low(attend(queries, keys, values, validity)).reshape(length, -1)
    hidden_state = inputs + low_back(product(attention, output_projection_weight))
    ff_in = low(layer_norm(hidden_state, feedforward_gain))
    activated = low(jax.nn.gelu(low_back(product(ff_in, up_projection_weight))))
    output = hidden_state + product(activated, down_projection_weight)
    reduced = length // 3
    stacked = memory[:3 * reduced].reshape(reduced, 3 * D)
    appended = low_back(low(product(stacked, squeeze_w.reshape(3 * D, D))))
    fixed_normed = low(layer_norm(fixed_inputs, fixed_gain))
    fixed_queries = to_heads(low(product(fixed_normed, fixed_query)))
    fixed_memory = low(layer_norm(memory, fixed_gain))
    memory_keys = to_heads(low(product(fixed_memory, fixed_key)))
    memory_values = to_heads(low(product(fixed_memory, fixed_value)))
    appended_rows = low(layer_norm(appended, fixed_gain))
    appended_keys = to_heads(low_back(low(product(appended_rows, fixed_key))))
    appended_values = to_heads(low_back(low(product(appended_rows, fixed_value))))
    rebuilt_memory = attend(fixed_queries, memory_keys, memory_values, None)
    rebuilt_squeezed = attend(fixed_queries, appended_keys, appended_values, None)
    differ = rebuilt_memory - rebuilt_squeezed
    return (output, appended, jnp.sum(differ * differ))

def run_group(params, fixed, inputs, memory, older, offsets, fixed_inputs):
    return lax.map(jax.checkpoint(partial(sequence_pass, params, fixed)), (inputs, memory, older, offsets, fixed_inputs))

def widen(array):
    return array.astype(jnp.float32)

def reference(inputs_short, memory_short, compressed_short, offsets_short, inputs_long, memory_long, compressed_long, offsets_long, query_weight, key_weight, value_weight, out_weight, up_weight, down_weight, compress_weight, attention_gain, feedforward_gain, cotangent_short, cotangent_long):
    params = tuple((widen(weight) for weight in (query_weight, key_weight, value_weight, out_weight, up_weight, down_weight, compress_weight, attention_gain, feedforward_gain)))
    fixed = (params[0], params[1], params[2], params[7])
    memory_s, older_s = (widen(memory_short), widen(compressed_short))
    memory_l, older_l = (widen(memory_long), widen(compressed_long))
    fixed_short = widen(inputs_short)
    fixed_long = widen(inputs_long)

    def forward(weights, short_inputs, long_inputs):
        short_out, short_added, short_square = run_group(weights, fixed, short_inputs, memory_s, older_s, offsets_short, fixed_short)
        long_out, long_added, long_square = run_group(weights, fixed, long_inputs, memory_l, older_l, offsets_long, fixed_long)
        return (short_out, long_out, short_added, long_added, jnp.sum(short_square) + jnp.sum(long_square))
    results, pullback = jax.vjp(forward, params, widen(inputs_short), widen(inputs_long))
    cotangents = (widen(cotangent_short), widen(cotangent_long), jnp.zeros_like(results[2]), jnp.zeros_like(results[3]), jnp.asarray(rebuild_weight, jnp.float32))
    grad_params, grad_short, grad_long = pullback(cotangents)
    loss = results[4] / ROWS_ALL
    return (results[0].astype(jnp.bfloat16), results[1].astype(jnp.bfloat16), grad_short, grad_long, results[2].astype(jnp.bfloat16), results[3].astype(jnp.bfloat16), grad_params[0], grad_params[1], grad_params[2], grad_params[3], grad_params[4], grad_params[5], grad_params[6], grad_params[7], grad_params[8], loss)
```

```python
import jax
import jax.numpy as jnp
from jax import lax
from jax.sharding import PartitionSpec as P

HEAD_SIZE = 128


epsilon = 1e-05
rebuild_weight = 256.0
masked_value = -1e30

AXES = ("dp", "tensor")


class Layout:
    def __init__(self):
        self.dp, self.tensor = lax.axis_size("dp"), lax.axis_size("tensor")
        self.half = self.tensor // 2
        self.columns = self.dp // 2
        place, plane = lax.axis_index("dp"), lax.axis_index("tensor")
        self.core, self.column = place % 2, place // 2
        self.upper, self.lower = plane // self.half, plane % self.half
        self.bits = [bit for bit in range(self.half.bit_length() - 1)]
        self.shard = self.core * self.half + self.lower
        self.groups = [[2 * c + core for c in range(self.columns)] for core in range(2)]

    def permute(self, value, move):
        pairs = []
        for d in range(self.dp):
            for t in range(self.tensor):
                column, core, upper, lower = move(d // 2, d % 2, t // self.half, t % self.half)
                pairs.append((d * self.tensor + t, (2 * column + core) * self.tensor + upper * self.half + lower))
        return jax.tree.map(lambda part: lax.ppermute(part, AXES, pairs), value)

    def swap(self, value):
        return self.permute(value, lambda p, c, h, a: (p, h, c, a))

    def flip_core(self, value):
        return self.permute(value, lambda p, c, h, a: (p, 1 - c, h, a))

    def flip_lower(self, value, bit):
        return self.permute(value, lambda p, c, h, a: (p, c, h, a ^ (1 << bit)))

    def gather(self, value, axis):
        def join(own, other, second):
            return jnp.where(
                second, jnp.concatenate([other, own], axis), jnp.concatenate([own, other], axis)
            )

        for bit in self.bits:
            value = join(value, self.flip_lower(value, bit), (self.lower >> bit) % 2 == 1)
        return join(value, self.flip_core(value), self.core == 1)

    def scatter(self, value, axis):
        def part(value, index):
            extent = value.shape[axis] // 2
            return lax.dynamic_slice_in_dim(value, index * extent, extent, axis)

        def step(value, index, exchange):
            other = exchange(part(value, 1 - index).astype(jnp.bfloat16))
            return part(value, index).astype(jnp.float32) + other.astype(jnp.float32)

        value = step(value, self.core, self.flip_core)
        for bit in reversed(self.bits):
            value = step(value, (self.lower >> bit) % 2, lambda v, bit=bit: self.flip_lower(v, bit))
        return value

    def total(self, value):
        for exchange in [self.flip_core] + [
            lambda v, bit=bit: self.flip_lower(v, bit) for bit in self.bits
        ]:
            value = value.astype(jnp.bfloat16)
            value = value.astype(jnp.float32) + exchange(value).astype(jnp.float32)
        return value

    def weight(self, value):
        rows = value.shape[0] // self.columns
        mine = lax.dynamic_slice_in_dim(value, self.column * rows, rows, 0)
        return lax.all_gather(
            self.swap(mine), "dp", axis=0, tiled=True, axis_index_groups=self.groups
        )

    def grad(self, value):
        part = lax.psum_scatter(
            value.astype(jnp.bfloat16),
            "dp",
            scatter_dimension=0,
            tiled=True,
            axis_index_groups=self.groups,
        )
        rows = part.shape[0] // 2

        def eighth(index):
            return lax.dynamic_slice_in_dim(part, index * rows, rows, 0)

        other = self.permute(
            eighth(1 - self.upper),
            lambda p, c, h, a: (p, c, c, a) if c != h else (p, 1 - c, h, a),
        )
        own = self.permute(eighth(self.upper), lambda p, c, h, a: (p, h, c, a))
        summed = (own.astype(jnp.float32) + other.astype(jnp.float32)).astype(jnp.bfloat16)
        return lax.all_gather(summed, "dp", axis=0, tiled=True).astype(jnp.float32)


def normalize(rows):
    mean = jnp.mean(rows, -1, keepdims=True)
    centred = rows - mean
    inverse = lax.rsqrt(jnp.mean(centred * centred, -1, keepdims=True) + epsilon)
    return (centred * inverse, inverse)


def norm_back(grad_out, gain, unit, inverse):
    scaled = grad_out * gain
    return inverse * (
        scaled
        - jnp.mean(scaled, -1, keepdims=True)
        - unit * jnp.mean(scaled * unit, -1, keepdims=True)
    )


def to_heads(array, heads):
    return array.reshape(array.shape[0], heads, HEAD_SIZE)


def scores_of(query, key, validity):
    scores = jnp.einsum(
        "qhd,khd->hqk", query, key, preferred_element_type=jnp.float32
    ) * HEAD_SIZE ** (-0.5)
    if validity is None:
        return scores
    return jnp.where(validity[None], scores, masked_value)


def attend(query, key, value, validity):
    scores = scores_of(query, key, validity)
    top = jnp.max(scores, -1, keepdims=True)
    shifted = jnp.exp(scores - top)
    total = jnp.sum(shifted, -1, keepdims=True)
    probs = shifted / total
    result = jnp.einsum(
        "hqk,khd->qhd", probs.astype(jnp.bfloat16), value, preferred_element_type=jnp.float32
    )
    return (result, (top + jnp.log(total))[..., 0])


def attend_back(query, key, value, validity, log_total, grad_result):
    scores = scores_of(query, key, validity)
    probs = jnp.exp(scores - log_total[..., None])
    grad_value = jnp.einsum(
        "hqk,qhd->khd", probs.astype(jnp.bfloat16), grad_result, preferred_element_type=jnp.float32
    )
    grad_probs = jnp.einsum("qhd,khd->hqk", grad_result, value, preferred_element_type=jnp.float32)
    grad_scores = (probs * (grad_probs - jnp.sum(grad_probs * probs, -1, keepdims=True))).astype(
        jnp.bfloat16
    )
    scale = HEAD_SIZE ** (-0.5)
    grad_query = (
        jnp.einsum("hqk,khd->qhd", grad_scores, key, preferred_element_type=jnp.float32) * scale
    )
    grad_key = (
        jnp.einsum("hqk,qhd->khd", grad_scores, query, preferred_element_type=jnp.float32) * scale
    )
    return (grad_query, grad_key, grad_value)


def group_layer(layout, inputs, memory, older, offsets, cotangent, weights):
    inputs, memory, older, offsets, cotangent = layout.swap(
        (inputs, memory, older, offsets, cotangent)
    )
    (
        query_projection_weight,
        pairwise_weight,
        output_projection_weight,
        up_projection_weight,
        down_projection_weight,
        squeeze_w,
        attention_gain,
        feedforward_gain,
    ) = weights
    count = inputs.shape[0]
    width = inputs.shape[2]
    local_width = query_projection_weight.shape[1]
    heads = local_width // HEAD_SIZE
    unit_tokens, inverse_tokens = normalize(inputs.astype(jnp.float32))
    normed_tokens = (unit_tokens * attention_gain).astype(jnp.bfloat16)
    entire_tokens, whole_memory, whole_older = (
        layout.gather(normed_tokens, 1),
        layout.gather(memory, 1),
        layout.gather(older, 1),
    )
    length = entire_tokens.shape[1]
    reduced = length // 3
    unit_memory = normalize(jnp.concatenate([whole_older, whole_memory], 1).astype(jnp.float32))[0]
    memory_rows = (unit_memory * attention_gain).astype(jnp.bfloat16)
    incoming_keys = jnp.concatenate([memory_rows, entire_tokens], 1)
    queries = jnp.einsum(
        "qfc,cp->qfp", entire_tokens, query_projection_weight, preferred_element_type=jnp.float32
    ).astype(jnp.bfloat16)
    pairs = jnp.einsum(
        "qfc,cp->qfp", incoming_keys, pairwise_weight, preferred_element_type=jnp.float32
    ).astype(jnp.bfloat16)
    stacked = whole_memory[:, : 3 * reduced].reshape(count, reduced, 3 * width)
    appended_local = jnp.einsum(
        "srk,ke->sre",
        stacked,
        squeeze_w,
        preferred_element_type=jnp.float32,
    ).astype(jnp.bfloat16)
    appended_whole = layout.gather(appended_local, 2)
    unit_added, inverse_added = normalize(appended_whole.astype(jnp.float32))
    added_rows = (unit_added * attention_gain).astype(jnp.bfloat16)
    added_pairs = jnp.einsum(
        "srd,de->sre", added_rows, pairwise_weight, preferred_element_type=jnp.float32
    ).astype(jnp.bfloat16)
    query_place = jnp.arange(length)[:, None]
    key_place = jnp.arange(3 * length)[None, :]
    attended = []
    saved = []
    square_sum = jnp.zeros((), jnp.float32)
    for index in range(count):
        validity = jnp.where(
            key_place < 2 * length,
            key_place >= offsets[index],
            key_place - 2 * length <= query_place,
        )
        query = to_heads(queries[index], heads)
        key = to_heads(pairs[index, :, :local_width], heads)
        value = to_heads(pairs[index, :, local_width:], heads)
        added_key = to_heads(added_pairs[index, :, :local_width], heads)
        added_value = to_heads(added_pairs[index, :, local_width:], heads)
        result, log_main = attend(query, key, value, validity)
        rebuilt_memory, log_memory = attend(
            query, key[length : 2 * length], value[length : 2 * length], None
        )
        rebuilt_added, log_added = attend(query, added_key, added_value, None)
        differ = rebuilt_memory - rebuilt_added
        square_sum = square_sum + jnp.sum(differ * differ)
        attended.append(result.astype(jnp.bfloat16).reshape(length, local_width))
        saved.append(
            (validity, query, key, value, added_key, added_value, log_main, log_added, differ)
        )
    attention_complete = jnp.stack(attended)
    branch = layout.scatter(
        jnp.einsum(
            "owa,au->owu",
            attention_complete,
            output_projection_weight,
            preferred_element_type=jnp.float32,
        ).astype(jnp.bfloat16),
        1,
    )
    hidden_state = inputs.astype(jnp.float32) + branch
    unit_hidden, inverse_hidden = normalize(hidden_state)
    feedforward_entire = layout.gather((unit_hidden * feedforward_gain).astype(jnp.bfloat16), 1)
    preactivation = jnp.einsum(
        "urc,ch->urh", feedforward_entire, up_projection_weight, preferred_element_type=jnp.float32
    )
    activated, gelu_back = jax.vjp(jax.nn.gelu, preactivation)
    activated_reduced = activated.astype(jnp.bfloat16)
    feedforward = layout.scatter(
        jnp.einsum(
            "qer,rz->qez",
            activated_reduced,
            down_projection_weight,
            preferred_element_type=jnp.float32,
        ).astype(jnp.bfloat16),
        1,
    )
    output = (hidden_state + feedforward).astype(jnp.bfloat16)
    cotangent_entire = layout.gather(cotangent, 1)
    grad_down_w = jnp.einsum(
        "jkg,jki->gi", activated_reduced, cotangent_entire, preferred_element_type=jnp.float32
    )
    grad_activated = jnp.einsum(
        "vhr,mr->vhm", cotangent_entire, down_projection_weight, preferred_element_type=jnp.float32
    )
    grad_preactivation = gelu_back(grad_activated)[0].astype(jnp.bfloat16)
    grad_up_projection_weight = jnp.einsum(
        "aji,ajr->ir", feedforward_entire, grad_preactivation, preferred_element_type=jnp.float32
    )
    grad_ff = layout.scatter(
        jnp.einsum(
            "zar,vr->zav",
            grad_preactivation,
            up_projection_weight,
            preferred_element_type=jnp.float32,
        ).astype(jnp.bfloat16),
        1,
    )
    feed_gain_part = jnp.sum(grad_ff * unit_hidden, (0, 1))
    grad_hidden = cotangent.astype(jnp.float32) + norm_back(
        grad_ff, feedforward_gain, unit_hidden, inverse_hidden
    )
    grad_hidden_low = grad_hidden.astype(jnp.bfloat16)
    branch_entire = layout.gather(grad_hidden_low, 1)
    grad_out_w = jnp.einsum(
        "qnw,qny->wy", attention_complete, branch_entire, preferred_element_type=jnp.float32
    )
    grad_attention = jnp.einsum(
        "pcm,fm->pcf", branch_entire, output_projection_weight, preferred_element_type=jnp.float32
    ).astype(jnp.bfloat16)
    grad_queries = []
    grad_pairs = []
    grad_added = []
    for index in range(count):
        validity, query, key, value, added_key, added_value, log_main, log_added, differ = saved[
            index
        ]
        main_query, main_key, main_value = attend_back(
            query, key, value, validity, log_main, to_heads(grad_attention[index], heads)
        )
        pushed = -2.0 * rebuild_weight * differ
        unused_query, added_key_grad, added_value_grad = attend_back(
            query, added_key, added_value, None, log_added, pushed.astype(jnp.bfloat16)
        )
        grad_queries.append(main_query.astype(jnp.bfloat16).reshape(length, local_width))
        grad_pairs.append(
            jnp.concatenate(
                [
                    main_key.reshape(3 * length, local_width),
                    main_value.reshape(3 * length, local_width),
                ],
                1,
            ).astype(jnp.bfloat16)
        )
        grad_added.append(
            jnp.concatenate(
                [
                    added_key_grad.reshape(reduced, local_width),
                    added_value_grad.reshape(reduced, local_width),
                ],
                1,
            ).astype(jnp.bfloat16)
        )
    grad_query_complete = jnp.stack(grad_queries)
    grad_pair_complete = jnp.stack(grad_pairs)
    grad_added_all = jnp.stack(grad_added)
    grad_query_w = jnp.einsum(
        "pxv,pxf->vf", entire_tokens, grad_query_complete, preferred_element_type=jnp.float32
    )
    grad_pair_w = jnp.einsum(
        "pxv,pxf->vf", incoming_keys, grad_pair_complete, preferred_element_type=jnp.float32
    )
    grad_keys_in = jnp.einsum(
        "azr,pr->azp", grad_pair_complete, pairwise_weight, preferred_element_type=jnp.float32
    )
    grad_token_rows = grad_keys_in[:, 2 * length :] + jnp.einsum(
        "azr,pr->azp",
        grad_query_complete,
        query_projection_weight,
        preferred_element_type=jnp.float32,
    )
    attention_gain_part = jnp.sum(grad_keys_in[:, : 2 * length] * unit_memory, (0, 1))
    grad_added_norm = jnp.einsum(
        "sre,de->srd", grad_added_all, pairwise_weight, preferred_element_type=jnp.float32
    )
    added_full = layout.total(grad_added_norm)
    grad_appended = norm_back(added_full, attention_gain, unit_added, inverse_added).astype(
        jnp.bfloat16
    )
    grad_appended_local = lax.dynamic_slice_in_dim(
        grad_appended, layout.shard * local_width, local_width, 2
    )
    grad_squeeze_w = jnp.einsum(
        "srk,sre->ke", stacked, grad_appended_local, preferred_element_type=jnp.float32
    )
    grad_token_norm = layout.scatter(grad_token_rows.astype(jnp.bfloat16), 1)
    attention_gain_part = attention_gain_part + jnp.sum(grad_token_norm * unit_tokens, (0, 1))
    grad_inputs = grad_hidden + norm_back(
        grad_token_norm, attention_gain, unit_tokens, inverse_tokens
    )
    grads = (
        grad_query_w,
        grad_pair_w,
        grad_out_w,
        grad_up_projection_weight,
        grad_down_w,
        grad_squeeze_w,
    )
    output, grad_inputs, appended_local = layout.swap(
        (output, grad_inputs.astype(jnp.bfloat16), appended_local)
    )
    return (
        output,
        grad_inputs.astype(jnp.float32),
        appended_local,
        grads,
        attention_gain_part,
        feed_gain_part,
        square_sum,
        count * length,
    )


def per_device(
    inputs_short,
    memory_short,
    compressed_short,
    offsets_short,
    inputs_long,
    memory_long,
    compressed_long,
    offsets_long,
    query_weight,
    key_weight,
    value_weight,
    out_weight,
    up_weight,
    down_weight,
    compress_weight,
    attention_gain,
    feedforward_gain,
    cotangent_short,
    cotangent_long,
):
    layout = Layout()
    width, local_width = query_weight.shape
    qkv_weight = layout.weight(jnp.concatenate([query_weight, key_weight, value_weight], 1))
    weights = (
        qkv_weight[:, :local_width],
        qkv_weight[:, local_width:],
        layout.weight(out_weight),
        layout.weight(up_weight),
        layout.weight(down_weight),
        layout.weight(compress_weight.reshape(3 * width, local_width)),
        attention_gain,
        feedforward_gain,
    )
    short_result = group_layer(
        layout, inputs_short, memory_short, compressed_short, offsets_short, cotangent_short, weights
    )
    long_result = group_layer(
        layout, inputs_long, memory_long, compressed_long, offsets_long, cotangent_long, weights
    )
    summed = jax.tree.map(jnp.add, short_result[3], long_result[3])
    query_sum, pair_sum, out_sum, up_sum, down_sum, squeeze_sum = map(layout.grad, summed)
    summed = (
        query_sum,
        pair_sum[:, :local_width],
        pair_sum[:, local_width:],
        out_sum,
        up_sum,
        down_sum,
        squeeze_sum.reshape(3, width, local_width),
    )
    gain_one, gain_two, square_total = lax.psum(
        (
            short_result[4] + long_result[4],
            short_result[5] + long_result[5],
            short_result[6] + long_result[6],
        ),
        ("dp", "tensor"),
    )
    rows_all = (short_result[7] + long_result[7]) * lax.axis_size("dp")
    loss = square_total / rows_all
    return (
        short_result[0],
        long_result[0],
        short_result[1],
        long_result[1],
        short_result[2],
        long_result[2],
        summed[0],
        summed[1],
        summed[2],
        summed[3],
        summed[4],
        summed[5],
        summed[6],
        gain_one,
        gain_two,
        loss,
    )


def solution(mesh):
    in_specs = (
        P("dp", "tensor", None),
        P("dp", "tensor", None),
        P("dp", "tensor", None),
        P("dp"),
        P("dp", "tensor", None),
        P("dp", "tensor", None),
        P("dp", "tensor", None),
        P("dp"),
        P(None, "tensor"),
        P(None, "tensor"),
        P(None, "tensor"),
        P("tensor", None),
        P(None, "tensor"),
        P("tensor", None),
        P(None, None, "tensor"),
        P(),
        P(),
        P("dp", "tensor", None),
        P("dp", "tensor", None),
    )
    out_specs = (
        P("dp", "tensor", None),
        P("dp", "tensor", None),
        P("dp", "tensor", None),
        P("dp", "tensor", None),
        P("dp", None, "tensor"),
        P("dp", None, "tensor"),
        P(None, "tensor"),
        P(None, "tensor"),
        P(None, "tensor"),
        P("tensor", None),
        P(None, "tensor"),
        P("tensor", None),
        P(None, None, "tensor"),
        P(),
        P(),
        P(),
    )
    return jax.shard_map(
        per_device, mesh=mesh, in_specs=in_specs, out_specs=out_specs, check_vma=False
    )
```

```python
import functools

import jax
import jax.numpy as jnp
from jax import lax
from jax.experimental import pallas as pl
from jax.experimental.pallas import tpu as pltpu
from jax.sharding import PartitionSpec as P

HEAD_SIZE = 128
SCALE = HEAD_SIZE**-0.5
AXES = ("dp", "tensor")
NT = (((1,), (1,)), ((), ()))
TN = (((0,), (0,)), ((), ()))

epsilon = 1e-05
rebuild_weight = 256.0
masked_value = -1e30


class Layout:
    def __init__(self):
        self.dp, self.tensor = lax.axis_size("dp"), lax.axis_size("tensor")
        self.half = self.tensor // 2
        self.columns = self.dp // 2
        place, plane = lax.axis_index("dp"), lax.axis_index("tensor")
        self.core, self.column = place % 2, place // 2
        self.upper, self.lower = plane // self.half, plane % self.half
        self.shard = self.core * self.half + self.lower
        self.groups = [[2 * c + core for c in range(self.columns)] for core in range(2)]

    def permute(self, value, move):
        pairs = []
        for d in range(self.dp):
            for t in range(self.tensor):
                column, core, upper, lower = move(d // 2, d % 2, t // self.half, t % self.half)
                pairs.append(
                    (
                        d * self.tensor + t,
                        (2 * column + core) * self.tensor + upper * self.half + lower,
                    )
                )
        return jax.tree.map(lambda part: lax.ppermute(part, AXES, pairs), value)

    def swap(self, value):
        return self.permute(value, lambda p, c, h, a: (p, h, c, a))

    def flip(self, value, bit):
        if bit == self.half:
            return self.permute(value, lambda p, c, h, a: (p, 1 - c, h, a))
        return self.permute(value, lambda p, c, h, a: (p, c, h, a ^ bit))

    def gather(self, value):
        value = value[None]
        bit = 1
        while bit < self.tensor:
            value = jnp.concatenate([value, self.flip(value, bit)], 0)
            bit *= 2
        return value

    def scatter(self, value):
        bit = self.half
        while bit:
            value = value.astype(jnp.bfloat16)
            other = self.flip(value[bit:], bit)
            value = value[:bit].astype(jnp.float32) + other.astype(jnp.float32)
            bit //= 2
        return value[0]

    def total(self, value):
        bit = self.half
        while bit:
            value = value.astype(jnp.bfloat16)
            value = value.astype(jnp.float32) + self.flip(value, bit).astype(jnp.float32)
            bit //= 2
        return value

    def ordered(self, pieces, axis):
        return jnp.concatenate(
            [
                lax.dynamic_index_in_dim(pieces, self.shard ^ s, 0, False)
                for s in range(self.tensor)
            ],
            axis,
        )

    def weight(self, value):
        rows = value.shape[0] // self.columns
        mine = lax.dynamic_slice_in_dim(value, self.column * rows, rows, 0)
        return lax.all_gather(
            self.swap(mine), "dp", axis=0, tiled=True, axis_index_groups=self.groups
        )

    def grad(self, value):
        part = lax.psum_scatter(
            value.astype(jnp.bfloat16),
            "dp",
            scatter_dimension=0,
            tiled=True,
            axis_index_groups=self.groups,
        )
        rows = part.shape[0] // 2

        def eighth(index):
            return lax.dynamic_slice_in_dim(part, index * rows, rows, 0)

        other = self.permute(
            eighth(1 - self.upper),
            lambda p, c, h, a: (p, c, c, a) if c != h else (p, 1 - c, h, a),
        )
        own = self.permute(eighth(self.upper), lambda p, c, h, a: (p, h, c, a))
        summed = (own.astype(jnp.float32) + other.astype(jnp.float32)).astype(jnp.bfloat16)
        return lax.all_gather(summed, "dp", axis=0, tiled=True).astype(jnp.float32)


def normalize(rows):
    mean = jnp.mean(rows, -1, keepdims=True)
    centred = rows - mean
    inverse = lax.rsqrt(jnp.mean(centred * centred, -1, keepdims=True) + epsilon)
    return (centred * inverse, inverse)


def normed(rows, gain):
    return (normalize(rows.astype(jnp.float32))[0] * gain).astype(jnp.bfloat16)


def norm_back(grad_out, gain, unit, inverse):
    scaled = grad_out * gain
    return inverse * (
        scaled
        - jnp.mean(scaled, -1, keepdims=True)
        - unit * jnp.mean(scaled * unit, -1, keepdims=True)
    )


def matmul(left, right):
    return jnp.einsum("...k,kn->...n", left, right, preferred_element_type=jnp.float32)


def matmul_back(left, right):
    return jnp.einsum("...n,kn->...k", left, right, preferred_element_type=jnp.float32)


def outer(left, right):
    rows = left.reshape(-1, left.shape[-1])
    columns = right.reshape(-1, right.shape[-1])
    return jnp.einsum("rk,rn->kn", rows, columns, preferred_element_type=jnp.float32)


def dot(left, right, dims=(((1,), (0,)), ((), ()))):
    return lax.dot_general(left, right, dims, preferred_element_type=jnp.float32)


class Tiles:
    def __init__(self, me, pieces, rows, many):
        self.me, self.pieces, self.rows, self.many = me, pieces, rows, many

    def load(self, ref, tile, *where):
        parts = [ref[(self.me ^ (tile * self.many + i), *where)] for i in range(self.many)]
        return parts[0] if self.many == 1 else jnp.concatenate(parts, 0)

    def store(self, ref, tile, value, *where, add=False):
        for i in range(self.many):
            index = (self.me ^ (tile * self.many + i), *where)
            part = value[i * self.rows : (i + 1) * self.rows]
            ref[index] = ref[index] + part if add else part

    def chunks(self, ref):
        for first in range(0, self.pieces, self.many):
            part = ref[first : first + self.many, 0]
            yield first, part.reshape(self.many * self.rows, part.shape[-1])

    def place(self, first, axis):
        extent = self.many * self.rows
        index = lax.broadcasted_iota(jnp.int32, (1, extent) if axis else (extent, 1), axis)
        piece = lax.bitwise_xor(self.me, first + index // self.rows)
        return piece * self.rows + index % self.rows


def attend_kernel(
    reduced,
    many,
    me_ref,
    offsets_ref,
    q_ref,
    kx_ref,
    vx_ref,
    km_ref,
    vm_ref,
    kc_ref,
    vc_ref,
    ka_ref,
    va_ref,
    o_ref,
    push_ref,
    lse_ref,
    alse_ref,
    square_ref,
):
    seq, head, block = pl.program_id(0), pl.program_id(1), pl.program_id(2)
    pieces, _, rows, _ = q_ref.shape
    length, tile = pieces * rows, many * rows
    tiles = Tiles(me_ref[0], pieces, rows, many)
    offset = offsets_ref[seq]
    q = tiles.load(q_ref, block, 0)

    def fold(carry, scores, values):
        top, total, acc = carry
        fresh = jnp.maximum(top, jnp.max(scores, 1, keepdims=True))
        probs = jnp.exp(scores - fresh)
        keep = jnp.exp(top - fresh)
        total = total * keep + jnp.sum(probs, 1, keepdims=True)
        acc = acc * keep + dot(probs.astype(jnp.bfloat16), values)
        return fresh, total, acc

    def empty():
        return (
            jnp.full((tile, 1), masked_value, jnp.float32),
            jnp.zeros((tile, 1), jnp.float32),
            jnp.zeros((tile, HEAD_SIZE), jnp.float32),
        )

    main, memory = empty(), empty()
    for base, keys_ref, values_ref in ((0, kc_ref, vc_ref), (length, km_ref, vm_ref)):
        for (first, keys), (_, values) in zip(tiles.chunks(keys_ref), tiles.chunks(values_ref)):
            scores = dot(q, keys, NT) * SCALE
            if base:
                memory = fold(memory, scores, values)
            allowed = tiles.place(first, 1) + base >= offset
            main = fold(main, jnp.where(allowed, scores, masked_value), values)

    def below(index, carry):
        keys, values = tiles.load(kx_ref, index, 0), tiles.load(vx_ref, index, 0)
        return fold(carry, dot(q, keys, NT) * SCALE, values)

    main = lax.fori_loop(0, block, below, main)
    scores = dot(q, tiles.load(kx_ref, block, 0), NT) * SCALE
    causal = lax.broadcasted_iota(jnp.int32, (tile, tile), 1) <= lax.broadcasted_iota(
        jnp.int32, (tile, tile), 0
    )
    top, total, acc = fold(
        main, jnp.where(causal, scores, masked_value), tiles.load(vx_ref, block, 0)
    )
    tiles.store(o_ref, block, (acc / total).astype(jnp.bfloat16), 0)

    scores = dot(q, ka_ref[0], NT) * SCALE
    place = lax.broadcasted_iota(jnp.int32, (1, ka_ref.shape[1]), 1)
    atop, atotal, aacc = fold(
        empty(), jnp.where(place < reduced, scores, masked_value), va_ref[0]
    )
    differ = memory[2] / memory[1] - aacc / atotal
    tiles.store(push_ref, block, (-2.0 * rebuild_weight * differ).astype(jnp.bfloat16), 0)

    @pl.when((seq == 0) & (head == 0) & (block == 0))
    def _():
        square_ref[...] = jnp.zeros_like(square_ref)

    square_ref[...] += jnp.sum((differ * differ).reshape(tile // 8, 8, HEAD_SIZE), 0)

    def row(column):
        return jnp.transpose(jnp.broadcast_to(column, (tile, HEAD_SIZE)))[:1]

    lse_ref[0] = row(top + jnp.log(total))
    alse_ref[0] = row(atop + jnp.log(atotal))


def attention_specs(pieces, rows, heads, padded, tile):
    def whole(shift):
        return pl.BlockSpec(
            (pieces, 1, rows, HEAD_SIZE), lambda s, h, b, *_: (0, s, 0, h + shift * heads)
        )

    def added(shift):
        return pl.BlockSpec((1, padded, HEAD_SIZE), lambda s, h, b, *_: (s, 0, h + shift * heads))

    stat = pl.BlockSpec((1, 1, tile), lambda s, h, b, *_: (s * heads + h, 0, b))
    keys = [whole(0), whole(1), whole(2)] + [whole(0), whole(1)] * 2 + [added(0), added(1)]
    return whole, stat, keys


def tile_pieces(pieces, rows):
    return min(pieces, max(1, 512 // rows))


def attend(me, offsets, triples, memory, older, added, reduced):
    pieces, count, rows, _ = triples.shape
    heads = memory.shape[-1] // (2 * HEAD_SIZE)
    padded, length = added.shape[1], pieces * rows
    many = tile_pieces(pieces, rows)
    whole, stat, keys = attention_specs(pieces, rows, heads, padded, many * rows)
    tokens = jax.ShapeDtypeStruct((pieces, count, rows, heads * HEAD_SIZE), jnp.bfloat16)
    stats = jax.ShapeDtypeStruct((count * heads, 1, length), jnp.float32)
    work = count * heads * length * (3 * length + padded)
    return pl.pallas_call(
        functools.partial(attend_kernel, reduced, many),
        grid_spec=pltpu.PrefetchScalarGridSpec(
            num_scalar_prefetch=2,
            grid=(count, heads, pieces // many),
            in_specs=keys,
            out_specs=[
                whole(0),
                whole(0),
                stat,
                stat,
                pl.BlockSpec((8, HEAD_SIZE), lambda *_: (0, 0)),
            ],
        ),
        out_shape=[tokens, tokens, stats, stats, jax.ShapeDtypeStruct((8, HEAD_SIZE), jnp.float32)],
        cost_estimate=pl.CostEstimate(
            flops=work * 4 * HEAD_SIZE * 2, bytes_accessed=work // 64, transcendentals=work
        ),
        name="attend",
    )(me, offsets, triples, triples, triples, memory, memory, older, older, added, added)


def attend_back_kernel(
    reduced,
    many,
    heads,
    me_ref,
    offsets_ref,
    q_ref,
    kx_ref,
    vx_ref,
    km_ref,
    vm_ref,
    kc_ref,
    vc_ref,
    ka_ref,
    va_ref,
    o_ref,
    do_ref,
    push_ref,
    lse_ref,
    alse_ref,
    dx_ref,
    dm_ref,
    dc_ref,
    da_ref,
    kx_acc,
    vx_acc,
    km_acc,
    vm_acc,
    kc_acc,
    vc_acc,
    ka_acc,
    va_acc,
):
    seq, head, block = pl.program_id(0), pl.program_id(1), pl.program_id(2)
    pieces, _, rows, _ = q_ref.shape
    length, tile = pieces * rows, many * rows
    tiles = Tiles(me_ref[0], pieces, rows, many)
    offset = offsets_ref[seq]
    q, grad = tiles.load(q_ref, block, 0), tiles.load(do_ref, block, 0)

    @pl.when(block == 0)
    def _():
        for ref in (kx_acc, vx_acc, km_acc, vm_acc, kc_acc, vc_acc, ka_acc, va_acc):
            ref[...] = jnp.zeros_like(ref)

    lse = lse_ref[0]
    both = grad.astype(jnp.float32) * tiles.load(o_ref, block, 0).astype(jnp.float32)
    delta = jnp.sum(jnp.transpose(both), 0, keepdims=True)

    def piece(keys, values, allowed):
        scores = dot(keys, q, NT) * SCALE
        if allowed is not None:
            scores = jnp.where(allowed, scores, masked_value)
        probs = jnp.exp(scores - lse)
        dv = dot(probs.astype(jnp.bfloat16), grad)
        dp = dot(values, grad, NT)
        ds = (probs * (dp - delta)).astype(jnp.bfloat16)
        return dot(ds, q), dv, dot(ds, keys, TN)

    dq = jnp.zeros((tile, HEAD_SIZE), jnp.float32)
    for base, keys_ref, values_ref, k_acc, v_acc in (
        (0, kc_ref, vc_ref, kc_acc, vc_acc),
        (length, km_ref, vm_ref, km_acc, vm_acc),
    ):
        for (first, keys), (_, values) in zip(tiles.chunks(keys_ref), tiles.chunks(values_ref)):
            dk, dv, part = piece(keys, values, tiles.place(first, 0) + base >= offset)
            k_acc[first : first + many] += dk.reshape(many, rows, HEAD_SIZE)
            v_acc[first : first + many] += dv.reshape(many, rows, HEAD_SIZE)
            dq += part

    def token_tile(index, allowed, dq):
        dk, dv, part = piece(tiles.load(kx_ref, index, 0), tiles.load(vx_ref, index, 0), allowed)
        tiles.store(kx_acc, index, dk, add=True)
        tiles.store(vx_acc, index, dv, add=True)
        return dq + part

    dq = lax.fori_loop(0, block, lambda index, dq: token_tile(index, None, dq), dq)
    causal = lax.broadcasted_iota(jnp.int32, (tile, tile), 0) <= lax.broadcasted_iota(
        jnp.int32, (tile, tile), 1
    )
    dq = token_tile(block, causal, dq)

    def columns(kind):
        return pl.ds(pl.multiple_of((kind * heads + head) * HEAD_SIZE, HEAD_SIZE), HEAD_SIZE)

    tiles.store(dx_ref, block, (dq * SCALE).astype(jnp.bfloat16), 0, slice(None), columns(0))

    push = tiles.load(push_ref, block, 0)
    place = lax.broadcasted_iota(jnp.int32, (ka_ref.shape[1], 1), 0)
    scores = jnp.where(place < reduced, dot(ka_ref[0], q, NT) * SCALE, masked_value)
    probs = jnp.exp(scores - alse_ref[0])
    va_acc[...] += dot(probs.astype(jnp.bfloat16), push)
    dp = dot(va_ref[0], push, NT)
    shift = jnp.sum(probs * dp, 0, keepdims=True)
    ka_acc[...] += dot((probs * (dp - shift)).astype(jnp.bfloat16), q)

    @pl.when(block == pl.num_programs(2) - 1)
    def _():
        dx_ref[:, 0, :, columns(1)] = (kx_acc[...] * SCALE).astype(jnp.bfloat16)
        dx_ref[:, 0, :, columns(2)] = vx_acc[...].astype(jnp.bfloat16)
        dm_ref[:, 0, :, columns(0)] = (km_acc[...] * SCALE).astype(jnp.bfloat16)
        dm_ref[:, 0, :, columns(1)] = vm_acc[...].astype(jnp.bfloat16)
        dc_ref[:, 0, :, columns(0)] = (kc_acc[...] * SCALE).astype(jnp.bfloat16)
        dc_ref[:, 0, :, columns(1)] = vc_acc[...].astype(jnp.bfloat16)
        da_ref[0, :, columns(0)] = (ka_acc[...] * SCALE).astype(jnp.bfloat16)
        da_ref[0, :, columns(1)] = va_acc[...].astype(jnp.bfloat16)


def attend_back(
    me, offsets, triples, memory, older, added, out, grad, push, lse, alse, reduced
):
    pieces, count, rows, _ = triples.shape
    heads = memory.shape[-1] // (2 * HEAD_SIZE)
    padded, length = added.shape[1], pieces * rows
    many = tile_pieces(pieces, rows)
    whole, stat, keys = attention_specs(pieces, rows, heads, padded, many * rows)

    def result(like):
        if like.ndim == 3:
            return pl.BlockSpec((1, *like.shape[1:]), lambda s, h, b, *_: (s, 0, 0))
        return pl.BlockSpec((pieces, 1, rows, like.shape[-1]), lambda s, h, b, *_: (0, s, 0, 0))

    outputs = [triples, memory, older, added]
    work = count * heads * length * (3 * length + padded)
    return pl.pallas_call(
        functools.partial(attend_back_kernel, reduced, many, heads),
        grid_spec=pltpu.PrefetchScalarGridSpec(
            num_scalar_prefetch=2,
            grid=(count, heads, pieces // many),
            in_specs=keys + [whole(0)] * 3 + [stat, stat],
            out_specs=[result(like) for like in outputs],
            scratch_shapes=[pltpu.VMEM((pieces, rows, HEAD_SIZE), jnp.float32)] * 6
            + [pltpu.VMEM((padded, HEAD_SIZE), jnp.float32)] * 2,
        ),
        out_shape=[jax.ShapeDtypeStruct(like.shape, jnp.bfloat16) for like in outputs],
        cost_estimate=pl.CostEstimate(
            flops=work * 10 * HEAD_SIZE * 2, bytes_accessed=work // 32, transcendentals=work
        ),
        name="attend_back",
    )(
        me,
        offsets,
        triples,
        triples,
        triples,
        memory,
        memory,
        older,
        older,
        added,
        added,
        out,
        grad,
        push,
        lse,
        alse,
    )


def feedforward_kernel(chunk, rows_ref, grad_ref, up_ref, down_ref, *refs):
    if len(refs) > 4:
        up_in, down_in, out_ref, back_ref, gup_ref, gdown_ref, up_acc, down_acc = refs
    else:
        out_ref, back_ref, up_acc, down_acc = refs
    width, hidden = up_ref.shape
    rows, grad = rows_ref[...].reshape(-1, width), grad_ref[...].reshape(-1, width)
    out = back = None

    @pl.when(pl.program_id(0) == 0)
    def _():
        if len(refs) > 4:
            up_acc[...] = up_in[...]
            down_acc[...] = down_in[...]
        else:
            up_acc[...] = jnp.zeros_like(up_acc)
            down_acc[...] = jnp.zeros_like(down_acc)

    for start in range(0, hidden, chunk):
        part = slice(start, start + chunk)
        up, down = up_ref[:, part], down_ref[part]
        u = dot(rows, up)
        root, cube = 0.7978845608028654, 0.044715
        square = u * u
        bend = jnp.tanh(root * (u + cube * (square * u)))
        half = 0.5 * (1.0 + bend)
        active = (u * half).astype(jnp.bfloat16)
        slope = half + 0.5 * u * (1.0 - bend * bend) * (root * (1.0 + 3.0 * cube * square))
        pre = (dot(grad, down, NT) * slope).astype(jnp.bfloat16)
        fresh = dot(active, down)
        out = fresh if out is None else out + fresh
        fresh = dot(pre, up, NT)
        back = fresh if back is None else back + fresh
        down_acc[part] += dot(active, grad, TN)
        up_acc[:, part] += dot(rows, pre, TN)
    out_ref[...] = out.astype(jnp.bfloat16).reshape(out_ref.shape)
    back_ref[...] = back.astype(jnp.bfloat16).reshape(back_ref.shape)
    if len(refs) > 4:

        @pl.when(pl.program_id(0) == pl.num_programs(0) - 1)
        def _():
            gup_ref[...] = up_acc[...].astype(gup_ref.dtype)
            gdown_ref[...] = down_acc[...].astype(gdown_ref.dtype)


def feedforward(rows, grad, up, down, before):
    pieces, count, each, width = rows.shape
    hidden = up.shape[1]
    many = min(pieces, max(1, 512 // (count * each)))
    block = pl.BlockSpec((many, count, each, width), lambda s: (s, 0, 0, 0))

    def whole(like):
        return pl.BlockSpec(like.shape, lambda s: (0, 0), pipeline_mode=pl.Buffered(1))

    kind = jnp.bfloat16 if before else jnp.float32
    total = pieces * count * each
    return pl.pallas_call(
        functools.partial(feedforward_kernel, min(512, hidden)),
        grid=(pieces // many,),
        in_specs=[block, block, whole(up), whole(down)] + [whole(up), whole(down)] * bool(before),
        out_specs=[block, block, whole(up), whole(down)],
        scratch_shapes=[
            pltpu.VMEM(up.shape, jnp.float32),
            pltpu.VMEM(down.shape, jnp.float32),
        ]
        * bool(before),
        out_shape=[jax.ShapeDtypeStruct(rows.shape, jnp.bfloat16)] * 2
        + [jax.ShapeDtypeStruct(up.shape, kind), jax.ShapeDtypeStruct(down.shape, kind)],
        cost_estimate=pl.CostEstimate(
            flops=12 * total * width * hidden,
            bytes_accessed=8 * total * width + 12 * width * hidden,
            transcendentals=total * hidden,
        ),
        name="feedforward",
    )(rows, grad, up, down, *before)


def stack_kernel(reduced, me_ref, memory_ref, stacked_ref, rows_acc):
    pieces, _, rows, width = memory_ref.shape
    blocks, extent, lanes = rows_acc.shape
    padded = stacked_ref.shape[1]
    keep = lax.broadcasted_iota(jnp.int32, (padded, 1), 0) < reduced
    for block in range(blocks):
        columns = slice(block * lanes, (block + 1) * lanes)
        for piece in range(pieces):
            start = pl.multiple_of((me_ref[0] ^ piece) * rows, rows)
            rows_acc[block, pl.ds(start, rows)] = memory_ref[piece, 0, :, columns].astype(
                jnp.float32
            )
        rows_acc[block, pieces * rows :] = jnp.zeros((extent - pieces * rows, lanes), jnp.float32)
        for tap in range(3):
            taken = rows_acc[block, pl.ds(tap, padded, stride=3)]
            start = tap * width + block * lanes
            stacked_ref[0, :, start : start + lanes] = jnp.where(keep, taken, 0.0).astype(
                jnp.bfloat16
            )


def stack(me, memory, reduced, padded):
    pieces, count, rows, width = memory.shape
    return pl.pallas_call(
        functools.partial(stack_kernel, reduced),
        grid_spec=pltpu.PrefetchScalarGridSpec(
            num_scalar_prefetch=1,
            grid=(count,),
            in_specs=[pl.BlockSpec((pieces, 1, rows, width), lambda s, *_: (0, s, 0, 0))],
            out_specs=pl.BlockSpec((1, padded, 3 * width), lambda s, *_: (s, 0, 0)),
            scratch_shapes=[pltpu.VMEM((width // 128, 3 * padded, 128), jnp.float32)],
        ),
        out_shape=jax.ShapeDtypeStruct((count, padded, 3 * width), jnp.bfloat16),
        cost_estimate=pl.CostEstimate(
            flops=0, bytes_accessed=4 * memory.size, transcendentals=0
        ),
        name="stack_memory",
    )(me, memory)


class Group:
    def __init__(self, layout, inputs, memory, older, offsets, cotangent):
        self.layout, self.offsets = layout, layout.swap(offsets)
        self.me = layout.shard.reshape(1).astype(jnp.int32)
        self.count = inputs.shape[0]
        self.length = inputs.shape[1] * layout.tensor
        self.reduced = self.length // 3
        self.padded = -(-self.reduced // 128) * 128
        self.raw = layout.swap(jnp.stack([inputs, memory]))
        self.older = layout.swap(older)
        self.cotangent = layout.swap(cotangent)

    def enter(self, gain):
        layout = self.layout
        whole = layout.gather(self.raw)
        self.memory_rows = whole[:, 1]
        self.token_z = normed(whole[:, 0], gain)
        self.memory_z = normed(whole[:, 1], gain)
        self.older_z = normed(layout.gather(self.older), gain)
        self.stacked = stack(self.me, self.memory_rows, self.reduced, self.padded)

    def compress(self, squeeze, pair_weight, gain):
        layout = self.layout
        self.appended = matmul(self.stacked, squeeze).astype(jnp.bfloat16)
        whole = layout.ordered(layout.gather(self.appended), -1)
        self.added_unit, self.added_inverse = normalize(whole.astype(jnp.float32))
        rows = (self.added_unit * gain).astype(jnp.bfloat16)
        self.added = matmul(rows, pair_weight).astype(jnp.bfloat16)

    def attend(self, triple_weight, pair_weight):
        self.triples = matmul(self.token_z, triple_weight).astype(jnp.bfloat16)
        self.memory_pairs = matmul(self.memory_z, pair_weight).astype(jnp.bfloat16)
        self.older_pairs = matmul(self.older_z, pair_weight).astype(jnp.bfloat16)
        self.attention, self.push, self.lse, self.added_lse, squares = attend(
            self.me,
            self.offsets,
            self.triples,
            self.memory_pairs,
            self.older_pairs,
            self.added,
            self.reduced,
        )
        self.squares = jnp.sum(squares)

    def middle(self, out_weight, gain):
        layout = self.layout
        branch = layout.scatter(matmul(self.attention, out_weight))
        self.hidden = self.raw[0].astype(jnp.float32) + branch
        self.hidden_unit, self.hidden_inverse = normalize(self.hidden)
        self.feed_rows = layout.gather((self.hidden_unit * gain).astype(jnp.bfloat16))
        self.grad_rows = layout.gather(self.cotangent)

    def feed(self, up_weight, down_weight, before):
        out, back, grad_up, grad_down = feedforward(
            self.feed_rows, self.grad_rows, up_weight, down_weight, before
        )
        self.feed_out, self.feed_back = out, back
        return grad_up, grad_down

    def leave(self):
        layout = self.layout
        return layout.swap((self.hidden + layout.scatter(self.feed_out)).astype(jnp.bfloat16))

    def middle_back(self, gain, out_weight):
        layout = self.layout
        grad = layout.scatter(self.feed_back)
        self.feed_gain = jnp.sum(grad * self.hidden_unit, (0, 1))
        self.grad_hidden = self.cotangent.astype(jnp.float32) + norm_back(
            grad, gain, self.hidden_unit, self.hidden_inverse
        )
        whole = layout.gather(self.grad_hidden.astype(jnp.bfloat16))
        self.grad_attention = matmul_back(whole, out_weight).astype(jnp.bfloat16)
        return outer(self.attention, whole)

    def attend_back(self):
        self.grad_triples, self.grad_memory, self.grad_older, self.grad_added = attend_back(
            self.me,
            self.offsets,
            self.triples,
            self.memory_pairs,
            self.older_pairs,
            self.added,
            self.attention,
            self.grad_attention,
            self.push,
            self.lse,
            self.added_lse,
            self.reduced,
        )

    def compress_back(self, pair_weight, gain):
        layout = self.layout
        grad = layout.total(matmul_back(self.grad_added, pair_weight))
        grad = norm_back(grad, gain, self.added_unit, self.added_inverse).astype(jnp.bfloat16)
        extent = self.appended.shape[2]
        mine = lax.dynamic_slice_in_dim(grad, layout.shard * extent, extent, 2)
        return outer(self.stacked, mine)

    def enter_back(self, triple_weight, gain):
        layout = self.layout
        grad = layout.scatter(matmul_back(self.grad_triples, triple_weight))
        unit, inverse = normalize(self.raw[0].astype(jnp.float32))
        full = self.grad_hidden + norm_back(grad, gain, unit, inverse)
        return layout.swap(full.astype(jnp.bfloat16)).astype(jnp.float32)

    def projection_grads(self):
        width = self.grad_triples.shape[-1] // 3
        triple = outer(self.token_z, self.grad_triples)
        pair = outer(self.memory_z, self.grad_memory) + outer(self.older_z, self.grad_older)
        return triple + jnp.pad(pair, ((0, 0), (width, 0)))

    def leave_appended(self):
        return self.layout.swap(self.appended)[:, : self.reduced]


def per_device(
    inputs_short,
    memory_short,
    compressed_short,
    offsets_short,
    inputs_long,
    memory_long,
    compressed_long,
    offsets_long,
    query_weight,
    key_weight,
    value_weight,
    out_weight,
    up_weight,
    down_weight,
    compress_weight,
    attention_gain,
    feedforward_gain,
    cotangent_short,
    cotangent_long,
):
    layout = Layout()
    width, local_width = query_weight.shape
    short = Group(
        layout, inputs_short, memory_short, compressed_short, offsets_short, cotangent_short
    )
    long = Group(layout, inputs_long, memory_long, compressed_long, offsets_long, cotangent_long)
    groups = (short, long)
    triple_weight = layout.weight(jnp.concatenate([query_weight, key_weight, value_weight], 1))
    pair_weight = triple_weight[:, local_width:]
    squeeze = layout.weight(compress_weight.reshape(3 * width, local_width))
    output_weight = layout.weight(out_weight)
    up, down = layout.weight(up_weight), layout.weight(down_weight)

    before = ()
    grad_out = grad_squeeze = grad_triple = 0.0
    for group in groups:
        group.enter(attention_gain)
        group.compress(squeeze, pair_weight, attention_gain)
        group.attend(triple_weight, pair_weight)
        group.middle(output_weight, feedforward_gain)
        before = group.feed(up, down, before)
        grad_out += group.middle_back(feedforward_gain, output_weight)
        group.attend_back()
        grad_squeeze += group.compress_back(pair_weight, attention_gain)
        grad_triple += group.projection_grads()
    up_sum, down_sum = map(layout.grad, before)
    out_sum = layout.grad(grad_out)
    squeeze_sum = layout.grad(grad_squeeze).reshape(3, width, local_width)
    triple_sum = layout.grad(grad_triple)
    attention_part = (
        jnp.sum(grad_triple * triple_weight.astype(jnp.float32), 1) / attention_gain
    )
    gain_one, gain_two, square_total = lax.psum(
        (
            attention_part,
            short.feed_gain + long.feed_gain,
            short.squares + long.squares,
        ),
        AXES,
    )
    rows_all = sum(group.count * group.length for group in groups) * layout.dp
    return (
        short.leave(),
        long.leave(),
        short.enter_back(triple_weight, attention_gain),
        long.enter_back(triple_weight, attention_gain),
        short.leave_appended(),
        long.leave_appended(),
        triple_sum[:, :local_width],
        triple_sum[:, local_width : 2 * local_width],
        triple_sum[:, 2 * local_width :],
        out_sum,
        up_sum,
        down_sum,
        squeeze_sum,
        gain_one,
        gain_two,
        square_total / rows_all,
    )


def solution(mesh):
    in_specs = (
        P("dp", "tensor", None),
        P("dp", "tensor", None),
        P("dp", "tensor", None),
        P("dp"),
        P("dp", "tensor", None),
        P("dp", "tensor", None),
        P("dp", "tensor", None),
        P("dp"),
        P(None, "tensor"),
        P(None, "tensor"),
        P(None, "tensor"),
        P("tensor", None),
        P(None, "tensor"),
        P("tensor", None),
        P(None, None, "tensor"),
        P(),
        P(),
        P("dp", "tensor", None),
        P("dp", "tensor", None),
    )
    out_specs = (
        P("dp", "tensor", None),
        P("dp", "tensor", None),
        P("dp", "tensor", None),
        P("dp", "tensor", None),
        P("dp", None, "tensor"),
        P("dp", None, "tensor"),
        P(None, "tensor"),
        P(None, "tensor"),
        P(None, "tensor"),
        P("tensor", None),
        P(None, "tensor"),
        P("tensor", None),
        P(None, None, "tensor"),
        P(),
        P(),
        P(),
    )
    return jax.shard_map(
        per_device, mesh=mesh, in_specs=in_specs, out_specs=out_specs, check_vma=False
    )
```

```python
import functools

import jax
import jax.numpy as jnp
from jax import lax
from jax.experimental import pallas as pl
from jax.experimental.pallas import tpu as pltpu
from jax.sharding import PartitionSpec as P

HEAD_SIZE = 128
SCALE = HEAD_SIZE**-0.5
AXES = ("dp", "tensor")
NT = (((1,), (1,)), ((), ()))
TN = (((0,), (0,)), ((), ()))

epsilon = 1e-05
rebuild_weight = 256.0
masked_value = -1e30


class Layout:
    def __init__(self):
        self.dp, self.tensor = lax.axis_size("dp"), lax.axis_size("tensor")
        self.half = self.tensor // 2
        self.columns = self.dp // 2
        place, plane = lax.axis_index("dp"), lax.axis_index("tensor")
        self.core, self.column = place % 2, place // 2
        self.upper, self.lower = plane // self.half, plane % self.half
        self.shard = self.core * self.half + self.lower
        self.groups = [[2 * c + core for c in range(self.columns)] for core in range(2)]

    def permute(self, value, move):
        pairs = []
        for d in range(self.dp):
            for t in range(self.tensor):
                column, core, upper, lower = move(d // 2, d % 2, t // self.half, t % self.half)
                pairs.append(
                    (
                        d * self.tensor + t,
                        (2 * column + core) * self.tensor + upper * self.half + lower,
                    )
                )
        return jax.tree.map(lambda part: lax.ppermute(part, AXES, pairs), value)

    def swap(self, value):
        return self.permute(value, lambda p, c, h, a: (p, h, c, a))

    def flip(self, value, bit):
        if bit == self.half:
            return self.permute(value, lambda p, c, h, a: (p, 1 - c, h, a))
        return self.permute(value, lambda p, c, h, a: (p, c, h, a ^ bit))

    def gather(self, value):
        value = value[None]
        bit = 1
        while bit < self.tensor:
            value = jnp.concatenate([value, self.flip(value, bit)], 0)
            bit *= 2
        return value

    def scatter(self, value):
        bit = self.half
        while bit:
            value = value.astype(jnp.bfloat16)
            other = self.flip(value[bit:], bit)
            value = value[:bit].astype(jnp.float32) + other.astype(jnp.float32)
            bit //= 2
        return value[0]

    def total(self, value):
        for axis, extent in zip(AXES, (self.dp, self.tensor)):
            bit = 1
            while bit < extent:
                pairs = [(i, i ^ bit) for i in range(extent)]
                value = value + lax.ppermute(value, axis, pairs)
                bit *= 2
        return value

    def ordered(self, pieces, axis):
        return jnp.concatenate(
            [
                lax.dynamic_index_in_dim(pieces, self.shard ^ s, 0, False)
                for s in range(self.tensor)
            ],
            axis,
        )

    def weight(self, value):
        rows = value.shape[0] // self.columns
        mine = lax.dynamic_slice_in_dim(value, self.column * rows, rows, 0)
        return lax.all_gather(
            self.swap(mine), "dp", axis=0, tiled=True, axis_index_groups=self.groups
        )

    def grad(self, value):
        part = lax.psum_scatter(
            value.astype(jnp.bfloat16),
            "dp",
            scatter_dimension=0,
            tiled=True,
            axis_index_groups=self.groups,
        )
        rows = part.shape[0] // 2

        def eighth(index):
            return lax.dynamic_slice_in_dim(part, index * rows, rows, 0)

        other = self.permute(
            eighth(1 - self.upper),
            lambda p, c, h, a: (p, c, c, a) if c != h else (p, 1 - c, h, a),
        )
        own = self.permute(eighth(self.upper), lambda p, c, h, a: (p, h, c, a))
        summed = (own.astype(jnp.float32) + other.astype(jnp.float32)).astype(jnp.bfloat16)
        mine = lax.all_gather(summed, "dp", axis_index_groups=self.groups)
        other = self.flip(mine, self.half)
        first = jnp.where(self.core == 0, mine, other)
        second = jnp.where(self.core == 0, other, mine)
        return jnp.stack([first, second], 1).reshape(value.shape).astype(jnp.float32)


def after(value, *done):
    return lax.optimization_barrier((value, done))[0]


def normalize(rows):
    mean = jnp.mean(rows, -1, keepdims=True)
    centred = rows - mean
    inverse = lax.rsqrt(jnp.mean(centred * centred, -1, keepdims=True) + epsilon)
    return (centred * inverse, inverse)


def normed(rows, gain):
    return (normalize(rows.astype(jnp.float32))[0] * gain).astype(jnp.bfloat16)


def norm_back(grad_out, gain, unit, inverse):
    scaled = grad_out * gain
    return inverse * (
        scaled
        - jnp.mean(scaled, -1, keepdims=True)
        - unit * jnp.mean(scaled * unit, -1, keepdims=True)
    )


def matmul(left, right):
    return jnp.einsum("...k,kn->...n", left, right, preferred_element_type=jnp.float32)


def matmul_back(left, right):
    return jnp.einsum("...n,kn->...k", left, right, preferred_element_type=jnp.float32)


def outer(left, right):
    rows = left.reshape(-1, left.shape[-1])
    columns = right.reshape(-1, right.shape[-1])
    return jnp.einsum("rk,rn->kn", rows, columns, preferred_element_type=jnp.float32)


def dot(left, right, dims=(((1,), (0,)), ((), ()))):
    return lax.dot_general(left, right, dims, preferred_element_type=jnp.float32)


class Tiles:
    def __init__(self, me, pieces, rows, many):
        self.me, self.pieces, self.rows, self.many = me, pieces, rows, many

    def load(self, ref, tile, *where):
        parts = [ref[(self.me ^ (tile * self.many + i), *where)] for i in range(self.many)]
        return parts[0] if self.many == 1 else jnp.concatenate(parts, 0)

    def store(self, ref, tile, value, *where, add=False):
        for i in range(self.many):
            index = (self.me ^ (tile * self.many + i), *where)
            part = value[i * self.rows : (i + 1) * self.rows]
            ref[index] = ref[index] + part if add else part

    def chunks(self, ref):
        for first in range(0, self.pieces, self.many):
            part = ref[first : first + self.many, 0]
            yield first, part.reshape(self.many * self.rows, part.shape[-1])

    def place(self, first, axis):
        extent = self.many * self.rows
        index = lax.broadcasted_iota(jnp.int32, (1, extent) if axis else (extent, 1), axis)
        piece = lax.bitwise_xor(self.me, first + index // self.rows)
        return piece * self.rows + index % self.rows


def attend_kernel(
    reduced,
    many,
    me_ref,
    offsets_ref,
    q_ref,
    kx_ref,
    vx_ref,
    km_ref,
    vm_ref,
    kc_ref,
    vc_ref,
    ka_ref,
    va_ref,
    o_ref,
    lse_ref,
    da_ref,
    square_ref,
    ka_acc,
    va_acc,
):
    seq, head, block = pl.program_id(0), pl.program_id(1), pl.program_id(2)
    heads = da_ref.shape[2] // (2 * HEAD_SIZE)
    pieces, _, rows, _ = q_ref.shape
    length, tile = pieces * rows, many * rows
    tiles = Tiles(me_ref[0], pieces, rows, many)
    offset = offsets_ref[seq]
    q = tiles.load(q_ref, block, 0)

    def fold(carry, scores, values):
        top, total, acc = carry
        fresh = jnp.maximum(top, jnp.max(scores, 1, keepdims=True))
        probs = jnp.exp(scores - fresh)
        keep = jnp.exp(top - fresh)
        total = total * keep + jnp.sum(probs, 1, keepdims=True)
        acc = acc * keep + dot(probs.astype(jnp.bfloat16), values)
        return fresh, total, acc

    def empty():
        return (
            jnp.full((tile, 1), masked_value, jnp.float32),
            jnp.zeros((tile, 1), jnp.float32),
            jnp.zeros((tile, HEAD_SIZE), jnp.float32),
        )

    main, memory = empty(), empty()
    for base, keys_ref, values_ref in ((0, kc_ref, vc_ref), (length, km_ref, vm_ref)):
        for (first, keys), (_, values) in zip(tiles.chunks(keys_ref), tiles.chunks(values_ref)):
            scores = dot(q, keys, NT) * SCALE
            if base:
                memory = fold(memory, scores, values)
            allowed = tiles.place(first, 1) + base >= offset
            main = fold(main, jnp.where(allowed, scores, masked_value), values)

    def below(index, carry):
        keys, values = tiles.load(kx_ref, index, 0), tiles.load(vx_ref, index, 0)
        return fold(carry, dot(q, keys, NT) * SCALE, values)

    main = lax.fori_loop(0, block, below, main)
    scores = dot(q, tiles.load(kx_ref, block, 0), NT) * SCALE
    causal = lax.broadcasted_iota(jnp.int32, (tile, tile), 1) <= lax.broadcasted_iota(
        jnp.int32, (tile, tile), 0
    )
    top, total, acc = fold(
        main, jnp.where(causal, scores, masked_value), tiles.load(vx_ref, block, 0)
    )
    tiles.store(o_ref, block, (acc / total).astype(jnp.bfloat16), 0)

    scores = dot(q, ka_ref[0], NT) * SCALE
    place = lax.broadcasted_iota(jnp.int32, (1, ka_ref.shape[1]), 1)
    atop, atotal, aacc = fold(
        empty(), jnp.where(place < reduced, scores, masked_value), va_ref[0]
    )
    differ = memory[2] / memory[1] - aacc / atotal
    push = (-2.0 * rebuild_weight * differ).astype(jnp.bfloat16)

    @pl.when((seq == 0) & (head == 0) & (block == 0))
    def _():
        square_ref[...] = jnp.zeros_like(square_ref)

    square_ref[...] += jnp.sum((differ * differ).reshape(tile // 8, 8, HEAD_SIZE), 0)

    def row(column):
        return jnp.transpose(jnp.broadcast_to(column, (tile, HEAD_SIZE)))[:1]

    lse_ref[0] = row(top + jnp.log(total))

    @pl.when(block == 0)
    def _():
        ka_acc[...] = jnp.zeros_like(ka_acc)
        va_acc[...] = jnp.zeros_like(va_acc)

    place = lax.broadcasted_iota(jnp.int32, (ka_ref.shape[1], 1), 0)
    scores = jnp.where(place < reduced, dot(ka_ref[0], q, NT) * SCALE, masked_value)
    probs = jnp.exp(scores - row(atop + jnp.log(atotal)))
    va_acc[...] += dot(probs.astype(jnp.bfloat16), push)
    dp = dot(va_ref[0], push, NT)
    shift = jnp.sum(probs * dp, 0, keepdims=True)
    ka_acc[...] += dot((probs * (dp - shift)).astype(jnp.bfloat16), q)

    @pl.when(block == pl.num_programs(2) - 1)
    def _():
        for kind, value in ((0, ka_acc[...] * SCALE), (1, va_acc[...])):
            start = pl.multiple_of((kind * heads + head) * HEAD_SIZE, HEAD_SIZE)
            da_ref[0, :, pl.ds(start, HEAD_SIZE)] = value.astype(jnp.bfloat16)


def attention_specs(pieces, rows, heads, tile):
    def whole(shift):
        return pl.BlockSpec(
            (pieces, 1, rows, HEAD_SIZE), lambda s, h, b, *_: (0, s, 0, h + shift * heads)
        )

    stat = pl.BlockSpec((1, 1, tile), lambda s, h, b, *_: (s * heads + h, 0, b))
    keys = [whole(0), whole(1), whole(2)] + [whole(0), whole(1)] * 2
    return whole, stat, keys


def tile_pieces(pieces, rows):
    return min(pieces, max(1, 512 // rows))


def attend(me, offsets, triples, memory, older, added, reduced):
    pieces, count, rows, _ = triples.shape
    heads = memory.shape[-1] // (2 * HEAD_SIZE)
    padded, length = added.shape[1], pieces * rows
    many = tile_pieces(pieces, rows)
    whole, stat, keys = attention_specs(pieces, rows, heads, many * rows)
    for shift in (0, heads):
        keys.append(
            pl.BlockSpec((1, padded, HEAD_SIZE), lambda s, h, b, *_, shift=shift: (s, 0, h + shift))
        )
    tokens = jax.ShapeDtypeStruct((pieces, count, rows, heads * HEAD_SIZE), jnp.bfloat16)
    stats = jax.ShapeDtypeStruct((count * heads, 1, length), jnp.float32)
    work = count * heads * length * (3 * length + padded)
    return pl.pallas_call(
        functools.partial(attend_kernel, reduced, many),
        grid_spec=pltpu.PrefetchScalarGridSpec(
            num_scalar_prefetch=2,
            grid=(count, heads, pieces // many),
            in_specs=keys,
            out_specs=[
                whole(0),
                stat,
                pl.BlockSpec((1, *added.shape[1:]), lambda s, h, b, *_: (s, 0, 0)),
                pl.BlockSpec((8, HEAD_SIZE), lambda *_: (0, 0)),
            ],
            scratch_shapes=[pltpu.VMEM((padded, HEAD_SIZE), jnp.float32)] * 2,
        ),
        out_shape=[
            tokens,
            stats,
            jax.ShapeDtypeStruct(added.shape, jnp.bfloat16),
            jax.ShapeDtypeStruct((8, HEAD_SIZE), jnp.float32),
        ],
        cost_estimate=pl.CostEstimate(
            flops=work * 4 * HEAD_SIZE * 2, bytes_accessed=work // 64, transcendentals=work
        ),
        name="attend",
    )(me, offsets, triples, triples, triples, memory, memory, older, older, added, added)


def attend_back_kernel(
    many,
    heads,
    me_ref,
    offsets_ref,
    q_ref,
    kx_ref,
    vx_ref,
    km_ref,
    vm_ref,
    kc_ref,
    vc_ref,
    o_ref,
    do_ref,
    lse_ref,
    dx_ref,
    dm_ref,
    dc_ref,
    kx_acc,
    vx_acc,
    km_acc,
    vm_acc,
    kc_acc,
    vc_acc,
):
    seq, head, block = pl.program_id(0), pl.program_id(1), pl.program_id(2)
    pieces, _, rows, _ = q_ref.shape
    length, tile = pieces * rows, many * rows
    tiles = Tiles(me_ref[0], pieces, rows, many)
    offset = offsets_ref[seq]
    q, grad = tiles.load(q_ref, block, 0), tiles.load(do_ref, block, 0)

    @pl.when(block == 0)
    def _():
        for ref in (kx_acc, vx_acc, km_acc, vm_acc, kc_acc, vc_acc):
            ref[...] = jnp.zeros_like(ref)

    lse = lse_ref[0]
    both = grad.astype(jnp.float32) * tiles.load(o_ref, block, 0).astype(jnp.float32)
    delta = jnp.sum(jnp.transpose(both), 0, keepdims=True)

    def piece(keys, values, allowed):
        scores = dot(keys, q, NT) * SCALE
        if allowed is not None:
            scores = jnp.where(allowed, scores, masked_value)
        probs = jnp.exp(scores - lse)
        dv = dot(probs.astype(jnp.bfloat16), grad)
        dp = dot(values, grad, NT)
        ds = (probs * (dp - delta)).astype(jnp.bfloat16)
        return dot(ds, q), dv, dot(ds, keys, TN)

    dq = jnp.zeros((tile, HEAD_SIZE), jnp.float32)
    for base, keys_ref, values_ref, k_acc, v_acc in (
        (0, kc_ref, vc_ref, kc_acc, vc_acc),
        (length, km_ref, vm_ref, km_acc, vm_acc),
    ):
        for (first, keys), (_, values) in zip(tiles.chunks(keys_ref), tiles.chunks(values_ref)):
            dk, dv, part = piece(keys, values, tiles.place(first, 0) + base >= offset)
            k_acc[first : first + many] += dk.reshape(many, rows, HEAD_SIZE)
            v_acc[first : first + many] += dv.reshape(many, rows, HEAD_SIZE)
            dq += part

    def token_tile(index, allowed, dq):
        dk, dv, part = piece(tiles.load(kx_ref, index, 0), tiles.load(vx_ref, index, 0), allowed)
        tiles.store(kx_acc, index, dk, add=True)
        tiles.store(vx_acc, index, dv, add=True)
        return dq + part

    dq = lax.fori_loop(0, block, lambda index, dq: token_tile(index, None, dq), dq)
    causal = lax.broadcasted_iota(jnp.int32, (tile, tile), 0) <= lax.broadcasted_iota(
        jnp.int32, (tile, tile), 1
    )
    dq = token_tile(block, causal, dq)

    def columns(kind):
        return pl.ds(pl.multiple_of((kind * heads + head) * HEAD_SIZE, HEAD_SIZE), HEAD_SIZE)

    tiles.store(dx_ref, block, (dq * SCALE).astype(jnp.bfloat16), 0, slice(None), columns(0))

    @pl.when(block == pl.num_programs(2) - 1)
    def _():
        dx_ref[:, 0, :, columns(1)] = (kx_acc[...] * SCALE).astype(jnp.bfloat16)
        dx_ref[:, 0, :, columns(2)] = vx_acc[...].astype(jnp.bfloat16)
        dm_ref[:, 0, :, columns(0)] = (km_acc[...] * SCALE).astype(jnp.bfloat16)
        dm_ref[:, 0, :, columns(1)] = vm_acc[...].astype(jnp.bfloat16)
        dc_ref[:, 0, :, columns(0)] = (kc_acc[...] * SCALE).astype(jnp.bfloat16)
        dc_ref[:, 0, :, columns(1)] = vc_acc[...].astype(jnp.bfloat16)


def attend_back(me, offsets, triples, memory, older, out, grad, lse):
    pieces, count, rows, _ = triples.shape
    heads = memory.shape[-1] // (2 * HEAD_SIZE)
    length = pieces * rows
    many = tile_pieces(pieces, rows)
    whole, stat, keys = attention_specs(pieces, rows, heads, many * rows)

    def result(like):
        return pl.BlockSpec((pieces, 1, rows, like.shape[-1]), lambda s, h, b, *_: (0, s, 0, 0))

    outputs = [triples, memory, older]
    work = count * heads * length * 3 * length
    return pl.pallas_call(
        functools.partial(attend_back_kernel, many, heads),
        grid_spec=pltpu.PrefetchScalarGridSpec(
            num_scalar_prefetch=2,
            grid=(count, heads, pieces // many),
            in_specs=keys + [whole(0), whole(0), stat],
            out_specs=[result(like) for like in outputs],
            scratch_shapes=[pltpu.VMEM((pieces, rows, HEAD_SIZE), jnp.float32)] * 6,
        ),
        out_shape=[jax.ShapeDtypeStruct(like.shape, jnp.bfloat16) for like in outputs],
        cost_estimate=pl.CostEstimate(
            flops=work * 10 * HEAD_SIZE * 2, bytes_accessed=work // 32, transcendentals=work
        ),
        name="attend_back",
    )(
        me,
        offsets,
        triples,
        triples,
        triples,
        memory,
        memory,
        older,
        older,
        out,
        grad,
        lse,
    )


def feedforward_kernel(chunk, rows_ref, grad_ref, up_ref, down_ref, *refs):
    if len(refs) > 4:
        up_in, down_in, out_ref, back_ref, gup_ref, gdown_ref, up_acc, down_acc = refs
    else:
        out_ref, back_ref, up_acc, down_acc = refs
    width, hidden = up_ref.shape
    rows, grad = rows_ref[...].reshape(-1, width), grad_ref[...].reshape(-1, width)
    out = back = None

    @pl.when(pl.program_id(0) == 0)
    def _():
        if len(refs) > 4:
            up_acc[...] = up_in[...]
            down_acc[...] = down_in[...]
        else:
            up_acc[...] = jnp.zeros_like(up_acc)
            down_acc[...] = jnp.zeros_like(down_acc)

    for start in range(0, hidden, chunk):
        part = slice(start, start + chunk)
        up, down = up_ref[:, part], down_ref[part]
        u = dot(rows, up)
        root, cube = 0.7978845608028654, 0.044715
        square = u * u
        bend = jnp.tanh(root * (u + cube * (square * u)))
        half = 0.5 * (1.0 + bend)
        active = (u * half).astype(jnp.bfloat16)
        slope = half + 0.5 * u * (1.0 - bend * bend) * (root * (1.0 + 3.0 * cube * square))
        pre = (dot(grad, down, NT) * slope).astype(jnp.bfloat16)
        fresh = dot(active, down)
        out = fresh if out is None else out + fresh
        fresh = dot(pre, up, NT)
        back = fresh if back is None else back + fresh
        down_acc[part] += dot(active, grad, TN)
        up_acc[:, part] += dot(rows, pre, TN)
    out_ref[...] = out.astype(jnp.bfloat16).reshape(out_ref.shape)
    back_ref[...] = back.astype(jnp.bfloat16).reshape(back_ref.shape)
    if len(refs) > 4:

        @pl.when(pl.program_id(0) == pl.num_programs(0) - 1)
        def _():
            gup_ref[...] = up_acc[...].astype(gup_ref.dtype)
            gdown_ref[...] = down_acc[...].astype(gdown_ref.dtype)


def feedforward(rows, grad, up, down, before):
    pieces, count, each, width = rows.shape
    hidden = up.shape[1]
    many = min(pieces, max(1, 512 // (count * each)))
    block = pl.BlockSpec((many, count, each, width), lambda s: (s, 0, 0, 0))

    def whole(like):
        return pl.BlockSpec(like.shape, lambda s: (0, 0), pipeline_mode=pl.Buffered(1))

    kind = jnp.bfloat16 if before else jnp.float32
    total = pieces * count * each
    return pl.pallas_call(
        functools.partial(feedforward_kernel, min(512, hidden)),
        grid=(pieces // many,),
        in_specs=[block, block, whole(up), whole(down)] + [whole(up), whole(down)] * bool(before),
        out_specs=[block, block, whole(up), whole(down)],
        scratch_shapes=[
            pltpu.VMEM(up.shape, jnp.float32),
            pltpu.VMEM(down.shape, jnp.float32),
        ]
        * bool(before),
        out_shape=[jax.ShapeDtypeStruct(rows.shape, jnp.bfloat16)] * 2
        + [jax.ShapeDtypeStruct(up.shape, kind), jax.ShapeDtypeStruct(down.shape, kind)],
        cost_estimate=pl.CostEstimate(
            flops=12 * total * width * hidden,
            bytes_accessed=8 * total * width + 12 * width * hidden,
            transcendentals=total * hidden,
        ),
        name="feedforward",
    )(rows, grad, up, down, *before)


def stack_kernel(reduced, me_ref, memory_ref, stacked_ref, rows_acc):
    pieces, _, rows, width = memory_ref.shape
    blocks, extent, lanes = rows_acc.shape
    padded = stacked_ref.shape[1]
    keep = lax.broadcasted_iota(jnp.int32, (padded, 1), 0) < reduced
    for block in range(blocks):
        columns = slice(block * lanes, (block + 1) * lanes)
        for piece in range(pieces):
            start = pl.multiple_of((me_ref[0] ^ piece) * rows, rows)
            rows_acc[block, pl.ds(start, rows)] = memory_ref[piece, 0, :, columns].astype(
                jnp.float32
            )
        rows_acc[block, pieces * rows :] = jnp.zeros((extent - pieces * rows, lanes), jnp.float32)
        for tap in range(3):
            taken = rows_acc[block, pl.ds(tap, padded, stride=3)]
            start = tap * width + block * lanes
            stacked_ref[0, :, start : start + lanes] = jnp.where(keep, taken, 0.0).astype(
                jnp.bfloat16
            )


def stack(me, memory, reduced, padded):
    pieces, count, rows, width = memory.shape
    return pl.pallas_call(
        functools.partial(stack_kernel, reduced),
        grid_spec=pltpu.PrefetchScalarGridSpec(
            num_scalar_prefetch=1,
            grid=(count,),
            in_specs=[pl.BlockSpec((pieces, 1, rows, width), lambda s, *_: (0, s, 0, 0))],
            out_specs=pl.BlockSpec((1, padded, 3 * width), lambda s, *_: (s, 0, 0)),
            scratch_shapes=[pltpu.VMEM((width // 128, 3 * padded, 128), jnp.float32)],
        ),
        out_shape=jax.ShapeDtypeStruct((count, padded, 3 * width), jnp.bfloat16),
        cost_estimate=pl.CostEstimate(
            flops=0, bytes_accessed=4 * memory.size, transcendentals=0
        ),
        name="stack_memory",
    )(me, memory)


def fetch_kernel(dp, tensor, activations, weights, *refs):
    half, columns = tensor // 2, dp // 2
    count = len(activations) + len(weights)
    inputs, outputs = refs[:count], refs[count : 2 * count]
    staged, (send, recv, stage_sem) = refs[2 * count : -3], refs[-3:]
    place, plane = lax.axis_index("dp"), lax.axis_index("tensor")
    core, column = place % 2, place // 2
    upper, lower = plane // half, plane % half
    stays = core == upper

    def other(column, core, upper, lower):
        return (2 * column + core, upper * half + lower)

    swapped = other(column, upper, core, lower)
    row_bits = [1 << i for i in range(half.bit_length() - 1)] + [half]
    column_bits = [1 << i for i in range(columns.bit_length() - 1)]

    def row_partner(bit):
        if bit == half:
            return other(column, 1 - core, upper, lower)
        return other(column, core, upper, lower ^ bit)

    def column_partner(bit):
        return other(column ^ bit, core, upper, lower)

    partners = [row_partner(bit) for bit in row_bits] + [column_partner(b) for b in column_bits]

    loads = []
    for i in range(len(weights)):
        source = inputs[len(activations) + i]
        rows = staged[i].shape[0]
        load = pltpu.make_async_copy(
            source.at[pl.ds(pl.multiple_of(column * rows, rows), rows)], staged[i], stage_sem.at[i]
        )
        load.start()
        loads.append(load)

    barrier = pltpu.get_barrier_semaphore()
    for partner in partners:
        pl.semaphore_signal(barrier, 1, device_id=partner, device_id_type=pl.DeviceIdType.MESH)

    @pl.when(stays)
    def _():
        pl.semaphore_wait(barrier, len(partners))

    @pl.when(jnp.logical_not(stays))
    def _():
        pl.semaphore_signal(barrier, 1, device_id=swapped, device_id_type=pl.DeviceIdType.MESH)
        pl.semaphore_wait(barrier, len(partners) + 1)

    for load in loads:
        load.wait()

    transfers = []
    for item in range(count):
        if item < len(activations):
            source, where, bits, partner = inputs[item], 0, row_bits, row_partner
        else:
            source, where = staged[item - len(activations)], column
            bits, partner = column_bits, column_partner
        transfers.append((item, source, where, bits, partner))
    ranks = activations + weights
    order = sorted(range(count), key=lambda item: ranks[item])

    def keep(item):
        _, source, where, _, _ = transfers[item]
        return pltpu.make_async_copy(source, outputs[item].at[where], recv.at[item, 0])

    def swap(item):
        _, source, where, _, _ = transfers[item]
        return pltpu.make_async_remote_copy(
            source,
            outputs[item].at[where],
            send.at[item, 0],
            recv.at[item, 0],
            device_id=swapped,
            device_id_type=pl.DeviceIdType.MESH,
        )

    def exchange(item, stage):
        _, _, where, bits, partner = transfers[item]
        bit = bits[stage - 1]
        if item < len(activations):
            source, target = outputs[item].at[pl.ds(0, bit)], outputs[item].at[pl.ds(bit, bit)]
        else:
            block = pl.ds(column // bit * bit, bit)
            source = target = outputs[item].at[block]
        return pltpu.make_async_remote_copy(
            source,
            target,
            send.at[item, stage],
            recv.at[item, stage],
            device_id=partner(bit),
            device_id_type=pl.DeviceIdType.MESH,
        )

    def begin(item):
        @pl.when(stays)
        def _():
            keep(item).start()

        @pl.when(jnp.logical_not(stays))
        def _():
            swap(item).start()

    ahead = 2
    for item in order[:ahead]:
        begin(item)

    depth = max(len(row_bits), len(column_bits))
    for tick in range(len(order) + depth):
        if tick + ahead < len(order):
            begin(order[tick + ahead])
        for stage in range(1, depth + 2):
            index = tick - stage + 1
            if not 0 <= index < len(order):
                continue
            item = order[index]
            bits = transfers[item][3]
            if stage == 1:

                @pl.when(stays)
                def _(item=item):
                    keep(item).wait()

                @pl.when(jnp.logical_not(stays))
                def _(item=item):
                    swap(item).wait_recv()

            elif stage <= len(bits) + 1:
                exchange(item, stage - 1).wait_recv()
            if stage <= len(bits):
                exchange(item, stage).start()

    @pl.when(jnp.logical_not(stays))
    def _():
        for item in order:
            swap(item).wait_send()

    for item in order:
        for stage in range(1, len(transfers[item][3]) + 1):
            exchange(item, stage).wait_send()


def fetch(layout, activations, weights):
    columns, tensor = layout.columns, layout.tensor
    arrays = [value for _, value in activations + weights]
    slices = [(value.shape[0] // columns, *value.shape[1:]) for _, value in weights]
    shapes = [(tensor, *value.shape) for _, value in activations] + [
        (columns, *part) for part in slices
    ]
    stages = tensor.bit_length() + columns.bit_length()
    results = pl.pallas_call(
        functools.partial(
            fetch_kernel,
            layout.dp,
            tensor,
            [rank for rank, _ in activations],
            [rank for rank, _ in weights],
        ),
        in_specs=[pl.BlockSpec(memory_space=pltpu.VMEM)] * len(activations)
        + [pl.BlockSpec(memory_space=pl.ANY)] * len(weights),
        out_specs=[pl.BlockSpec(memory_space=pl.ANY)] * len(arrays),
        out_shape=[jax.ShapeDtypeStruct(shape, jnp.bfloat16) for shape in shapes],
        scratch_shapes=[pltpu.VMEM(part, jnp.bfloat16) for part in slices]
        + [
            pltpu.SemaphoreType.DMA((len(arrays), stages)),
            pltpu.SemaphoreType.DMA((len(arrays), stages)),
            pltpu.SemaphoreType.DMA((len(weights),)),
        ],
        compiler_params=pltpu.CompilerParams(collective_id=0, has_side_effects=True),
        name="fetch",
    )(*arrays)
    whole = results[len(activations) :]
    return results[: len(activations)], [
        part.reshape(value.shape) for part, (_, value) in zip(whole, weights)
    ]


class Group:
    def __init__(self, layout, tokens, memory, older, cotangent, offsets):
        self.layout, self.offsets = layout, layout.swap(offsets)
        self.me = layout.shard.reshape(1).astype(jnp.int32)
        self.count = tokens.shape[1]
        self.length = tokens.shape[2] * layout.tensor
        self.reduced = self.length // 3
        self.padded = -(-self.reduced // 128) * 128
        self.token_rows, self.memory_rows, self.older_rows = tokens, memory, older
        self.grad_rows = cotangent
        self.raw, self.cotangent = tokens[0], cotangent[0]

    def enter(self, gain):
        self.token_z = normed(self.token_rows, gain)
        self.memory_z = normed(self.memory_rows, gain)
        self.older_z = normed(self.older_rows, gain)
        self.stacked = stack(self.me, self.memory_rows, self.reduced, self.padded)

    def compress(self, squeeze, pair_weight, gain):
        layout = self.layout
        self.appended = matmul(self.stacked, squeeze).astype(jnp.bfloat16)
        whole = layout.ordered(layout.gather(self.appended), -1)
        self.added_unit, self.added_inverse = normalize(whole.astype(jnp.float32))
        rows = (self.added_unit * gain).astype(jnp.bfloat16)
        self.added = matmul(rows, pair_weight).astype(jnp.bfloat16)

    def attend(self, triple_weight, pair_weight):
        self.triples = matmul(self.token_z, triple_weight).astype(jnp.bfloat16)
        self.memory_pairs = matmul(self.memory_z, pair_weight).astype(jnp.bfloat16)
        self.older_pairs = matmul(self.older_z, pair_weight).astype(jnp.bfloat16)
        self.attention, self.lse, self.grad_added, squares = attend(
            self.me,
            self.offsets,
            self.triples,
            self.memory_pairs,
            self.older_pairs,
            self.added,
            self.reduced,
        )
        self.squares = jnp.sum(squares)

    def middle(self, out_weight, gain):
        layout = self.layout
        branch = layout.scatter(matmul(self.attention, out_weight))
        self.hidden = self.raw.astype(jnp.float32) + branch
        self.hidden_unit, self.hidden_inverse = normalize(self.hidden)
        self.feed_rows = layout.gather((self.hidden_unit * gain).astype(jnp.bfloat16))

    def feed(self, up_weight, down_weight, before):
        out, back, grad_up, grad_down = feedforward(
            self.feed_rows, self.grad_rows, up_weight, down_weight, before
        )
        self.feed_out, self.feed_back = out, back
        return grad_up, grad_down

    def leave(self):
        layout = self.layout
        return layout.swap((self.hidden + layout.scatter(self.feed_out)).astype(jnp.bfloat16))

    def middle_back(self, gain, out_weight):
        layout = self.layout
        grad = layout.scatter(self.feed_back)
        self.feed_gain = jnp.sum(grad * self.hidden_unit, (0, 1))
        self.grad_hidden = self.cotangent.astype(jnp.float32) + norm_back(
            grad, gain, self.hidden_unit, self.hidden_inverse
        )
        whole = layout.gather(self.grad_hidden.astype(jnp.bfloat16))
        self.grad_attention = matmul_back(whole, out_weight).astype(jnp.bfloat16)
        return outer(self.attention, whole)

    def attend_back(self):
        self.grad_triples, self.grad_memory, self.grad_older = attend_back(
            self.me,
            self.offsets,
            self.triples,
            self.memory_pairs,
            self.older_pairs,
            self.attention,
            self.grad_attention,
            self.lse,
        )

    def compress_back(self, pair_weight, gain):
        layout = self.layout
        grad = matmul_back(self.grad_added, pair_weight)
        grad = norm_back(grad, gain, self.added_unit, self.added_inverse).astype(jnp.bfloat16)
        extent = self.appended.shape[2]
        pieces = jnp.stack(
            [
                lax.dynamic_slice_in_dim(grad, (layout.shard ^ j) * extent, extent, 2)
                for j in range(layout.tensor)
            ]
        )
        return outer(self.stacked, layout.scatter(pieces).astype(jnp.bfloat16))

    def enter_back(self, triple_weight, gain):
        layout = self.layout
        grad = layout.scatter(matmul_back(self.grad_triples, triple_weight))
        unit, inverse = normalize(self.raw.astype(jnp.float32))
        full = self.grad_hidden + norm_back(grad, gain, unit, inverse)
        return layout.swap(full.astype(jnp.bfloat16)).astype(jnp.float32)

    def projection_grads(self):
        width = self.grad_triples.shape[-1] // 3
        triple = outer(self.token_z, self.grad_triples)
        pair = outer(self.memory_z, self.grad_memory) + outer(self.older_z, self.grad_older)
        return triple + jnp.pad(pair, ((0, 0), (width, 0)))

    def leave_appended(self):
        return self.layout.swap(self.appended)[:, : self.reduced]


def per_device(
    inputs_short,
    memory_short,
    compressed_short,
    offsets_short,
    inputs_long,
    memory_long,
    compressed_long,
    offsets_long,
    query_weight,
    key_weight,
    value_weight,
    out_weight,
    up_weight,
    down_weight,
    compress_weight,
    attention_gain,
    feedforward_gain,
    cotangent_short,
    cotangent_long,
):
    layout = Layout()
    width, local_width = query_weight.shape
    rows, whole = fetch(
        layout,
        [
            (0, inputs_short),
            (1, memory_short),
            (2, compressed_short),
            (8, cotangent_short),
            (3, inputs_long),
            (4, memory_long),
            (5, compressed_long),
            (9, cotangent_long),
        ],
        [
            (1.1, query_weight),
            (1.2, key_weight),
            (1.3, value_weight),
            (2.1, compress_weight.reshape(3 * width, local_width)),
            (3.1, out_weight),
            (4.1, up_weight),
            (5.1, down_weight),
        ],
    )
    triple_weight = jnp.concatenate(whole[:3], 1)
    pair_weight = triple_weight[:, local_width:]
    squeeze, output_weight, up, down = whole[3:]
    short = Group(layout, *rows[:4], offsets_short)
    long = Group(layout, *rows[4:], offsets_long)
    groups = (short, long)

    before = ()
    grad_out = grad_squeeze = grad_triple = 0.0
    for group in groups:
        group.enter(attention_gain)
        group.compress(squeeze, pair_weight, attention_gain)
        group.attend(triple_weight, pair_weight)
        grad_squeeze += group.compress_back(pair_weight, attention_gain)
        group.middle(output_weight, feedforward_gain)
        before = group.feed(up, down, before)
        grad_out += group.middle_back(feedforward_gain, output_weight)
        group.attend_back()
        grad_triple += group.projection_grads()
    up_sum, down_sum = map(layout.grad, before)
    squeeze_sum = layout.grad(grad_squeeze).reshape(3, width, local_width)
    out_sum = layout.grad(grad_out)
    triple_sum = layout.grad(grad_triple)
    attention_part = (
        jnp.sum(grad_triple * triple_weight.astype(jnp.float32), 1) / attention_gain
    )
    sums = layout.total(
        jnp.concatenate(
            [
                attention_part,
                short.feed_gain + long.feed_gain,
                jnp.full((128,), short.squares + long.squares),
            ]
        ).reshape(-1, 128)
    ).reshape(-1)
    gain_one, gain_two, square_total = sums[:width], sums[width : 2 * width], sums[2 * width]
    rows_all = sum(group.count * group.length for group in groups) * layout.dp
    return (
        short.leave(),
        long.leave(),
        short.enter_back(triple_weight, attention_gain),
        long.enter_back(triple_weight, attention_gain),
        short.leave_appended(),
        long.leave_appended(),
        triple_sum[:, :local_width],
        triple_sum[:, local_width : 2 * local_width],
        triple_sum[:, 2 * local_width :],
        out_sum,
        up_sum,
        down_sum,
        squeeze_sum,
        gain_one,
        gain_two,
        square_total / rows_all,
    )


def solution(mesh):
    in_specs = (
        P("dp", "tensor", None),
        P("dp", "tensor", None),
        P("dp", "tensor", None),
        P("dp"),
        P("dp", "tensor", None),
        P("dp", "tensor", None),
        P("dp", "tensor", None),
        P("dp"),
        P(None, "tensor"),
        P(None, "tensor"),
        P(None, "tensor"),
        P("tensor", None),
        P(None, "tensor"),
        P("tensor", None),
        P(None, None, "tensor"),
        P(),
        P(),
        P("dp", "tensor", None),
        P("dp", "tensor", None),
    )
    out_specs = (
        P("dp", "tensor", None),
        P("dp", "tensor", None),
        P("dp", "tensor", None),
        P("dp", "tensor", None),
        P("dp", None, "tensor"),
        P("dp", None, "tensor"),
        P(None, "tensor"),
        P(None, "tensor"),
        P(None, "tensor"),
        P("tensor", None),
        P(None, "tensor"),
        P("tensor", None),
        P(None, None, "tensor"),
        P(),
        P(),
        P(),
    )
    return jax.shard_map(
        per_device, mesh=mesh, in_specs=in_specs, out_specs=out_specs, check_vma=False
    )
```

```python
import functools

import jax
import jax.numpy as jnp
from jax import lax
from jax.experimental import pallas as pl
from jax.experimental.pallas import tpu as pltpu
from jax.sharding import PartitionSpec as P

HEAD_SIZE = 128
SCALE = HEAD_SIZE**-0.5
AXES = ("dp", "tensor")
NT = (((1,), (1,)), ((), ()))
TN = (((0,), (0,)), ((), ()))

epsilon = 1e-05
rebuild_weight = 256.0
masked_value = -1e30


class Layout:
    def __init__(self):
        self.dp, self.tensor = lax.axis_size("dp"), lax.axis_size("tensor")
        self.half = self.tensor // 2
        self.columns = self.dp // 2
        place, plane = lax.axis_index("dp"), lax.axis_index("tensor")
        self.core, self.column = place % 2, place // 2
        self.upper, self.lower = plane // self.half, plane % self.half
        self.shard = self.core * self.half + self.lower
        self.groups = [[2 * c + core for c in range(self.columns)] for core in range(2)]

    def permute(self, value, move):
        pairs = []
        for d in range(self.dp):
            for t in range(self.tensor):
                column, core, upper, lower = move(d // 2, d % 2, t // self.half, t % self.half)
                pairs.append(
                    (
                        d * self.tensor + t,
                        (2 * column + core) * self.tensor + upper * self.half + lower,
                    )
                )
        return jax.tree.map(lambda part: lax.ppermute(part, AXES, pairs), value)

    def swap(self, value):
        return self.permute(value, lambda p, c, h, a: (p, h, c, a))

    def flip(self, value, bit):
        if bit == self.half:
            return self.permute(value, lambda p, c, h, a: (p, 1 - c, h, a))
        return self.permute(value, lambda p, c, h, a: (p, c, h, a ^ bit))

    def gather(self, value):
        value = value[None]
        bit = 1
        while bit < self.tensor:
            value = jnp.concatenate([value, self.flip(value, bit)], 0)
            bit *= 2
        return value

    def scatter(self, value):
        bit = self.half
        while bit:
            value = value.astype(jnp.bfloat16)
            other = self.flip(value[bit:], bit)
            value = value[:bit].astype(jnp.float32) + other.astype(jnp.float32)
            bit //= 2
        return value[0]

    def ordered(self, pieces, axis):
        return jnp.concatenate(
            [
                lax.dynamic_index_in_dim(pieces, self.shard ^ s, 0, False)
                for s in range(self.tensor)
            ],
            axis,
        )

    def split(self, grad):
        return grad.astype(jnp.bfloat16).reshape(self.columns, -1, grad.shape[1])

    def eighths(self, grad):
        return (self.columns, 2, grad.shape[0] // (2 * self.columns), grad.shape[1])


def normalize(rows):
    mean = jnp.mean(rows, -1, keepdims=True)
    centred = rows - mean
    inverse = lax.rsqrt(jnp.mean(centred * centred, -1, keepdims=True) + epsilon)
    return (centred * inverse, inverse)


def normed(rows, gain):
    return (normalize(rows.astype(jnp.float32))[0] * gain).astype(jnp.bfloat16)


def norm_back(grad_out, gain, unit, inverse):
    scaled = grad_out * gain
    return inverse * (
        scaled
        - jnp.mean(scaled, -1, keepdims=True)
        - unit * jnp.mean(scaled * unit, -1, keepdims=True)
    )


def matmul(left, right):
    return jnp.einsum("...k,kn->...n", left, right, preferred_element_type=jnp.float32)


def matmul_back(left, right):
    return jnp.einsum("...n,kn->...k", left, right, preferred_element_type=jnp.float32)


def outer(left, right):
    rows = left.reshape(-1, left.shape[-1])
    columns = right.reshape(-1, right.shape[-1])
    return jnp.einsum("rk,rn->kn", rows, columns, preferred_element_type=jnp.float32)


def dot(left, right, dims=(((1,), (0,)), ((), ()))):
    return lax.dot_general(left, right, dims, preferred_element_type=jnp.float32)


class Tiles:
    def __init__(self, me, pieces, rows, many):
        self.me, self.pieces, self.rows, self.many = me, pieces, rows, many

    def load(self, ref, tile, *where):
        parts = [ref[(self.me ^ (tile * self.many + i), *where)] for i in range(self.many)]
        return parts[0] if self.many == 1 else jnp.concatenate(parts, 0)

    def store(self, ref, tile, value, *where, add=False):
        for i in range(self.many):
            index = (self.me ^ (tile * self.many + i), *where)
            part = value[i * self.rows : (i + 1) * self.rows]
            ref[index] = ref[index] + part if add else part

    def chunks(self, ref):
        for first in range(0, self.pieces, self.many):
            part = ref[first : first + self.many, 0]
            yield first, part.reshape(self.many * self.rows, part.shape[-1])

    def place(self, first, axis):
        extent = self.many * self.rows
        index = lax.broadcasted_iota(jnp.int32, (1, extent) if axis else (extent, 1), axis)
        piece = lax.bitwise_xor(self.me, first + index // self.rows)
        return piece * self.rows + index % self.rows


def attend_kernel(
    reduced,
    many,
    me_ref,
    offsets_ref,
    q_ref,
    kx_ref,
    vx_ref,
    km_ref,
    vm_ref,
    kc_ref,
    vc_ref,
    ka_ref,
    va_ref,
    o_ref,
    lse_ref,
    da_ref,
    square_ref,
    ka_acc,
    va_acc,
):
    seq, head, block = pl.program_id(0), pl.program_id(1), pl.program_id(2)
    heads = da_ref.shape[2] // (2 * HEAD_SIZE)
    pieces, _, rows, _ = q_ref.shape
    length, tile = pieces * rows, many * rows
    tiles = Tiles(me_ref[0], pieces, rows, many)
    offset = offsets_ref[seq]
    q = tiles.load(q_ref, block, 0)

    def fold(carry, scores, values):
        top, total, acc = carry
        fresh = jnp.maximum(top, jnp.max(scores, 1, keepdims=True))
        probs = jnp.exp(scores - fresh)
        keep = jnp.exp(top - fresh)
        total = total * keep + jnp.sum(probs, 1, keepdims=True)
        acc = acc * keep + dot(probs.astype(jnp.bfloat16), values)
        return fresh, total, acc

    def empty():
        return (
            jnp.full((tile, 1), masked_value, jnp.float32),
            jnp.zeros((tile, 1), jnp.float32),
            jnp.zeros((tile, HEAD_SIZE), jnp.float32),
        )

    main, memory = empty(), empty()
    for base, keys_ref, values_ref in ((0, kc_ref, vc_ref), (length, km_ref, vm_ref)):
        for (first, keys), (_, values) in zip(tiles.chunks(keys_ref), tiles.chunks(values_ref)):
            scores = dot(q, keys, NT) * SCALE
            if base:
                memory = fold(memory, scores, values)
            allowed = tiles.place(first, 1) + base >= offset
            main = fold(main, jnp.where(allowed, scores, masked_value), values)

    def below(index, carry):
        keys, values = tiles.load(kx_ref, index, 0), tiles.load(vx_ref, index, 0)
        return fold(carry, dot(q, keys, NT) * SCALE, values)

    main = lax.fori_loop(0, block, below, main)
    scores = dot(q, tiles.load(kx_ref, block, 0), NT) * SCALE
    causal = lax.broadcasted_iota(jnp.int32, (tile, tile), 1) <= lax.broadcasted_iota(
        jnp.int32, (tile, tile), 0
    )
    top, total, acc = fold(
        main, jnp.where(causal, scores, masked_value), tiles.load(vx_ref, block, 0)
    )
    tiles.store(o_ref, block, (acc / total).astype(jnp.bfloat16), 0)

    scores = dot(q, ka_ref[0], NT) * SCALE
    place = lax.broadcasted_iota(jnp.int32, (1, ka_ref.shape[1]), 1)
    atop, atotal, aacc = fold(
        empty(), jnp.where(place < reduced, scores, masked_value), va_ref[0]
    )
    differ = memory[2] / memory[1] - aacc / atotal
    push = (-2.0 * rebuild_weight * differ).astype(jnp.bfloat16)

    @pl.when((seq == 0) & (head == 0) & (block == 0))
    def _():
        square_ref[...] = jnp.zeros_like(square_ref)

    square_ref[...] += jnp.sum((differ * differ).reshape(tile // 8, 8, HEAD_SIZE), 0)

    def row(column):
        return jnp.transpose(jnp.broadcast_to(column, (tile, HEAD_SIZE)))[:1]

    lse_ref[0] = row(top + jnp.log(total))

    @pl.when(block == 0)
    def _():
        ka_acc[...] = jnp.zeros_like(ka_acc)
        va_acc[...] = jnp.zeros_like(va_acc)

    place = lax.broadcasted_iota(jnp.int32, (ka_ref.shape[1], 1), 0)
    scores = jnp.where(place < reduced, dot(ka_ref[0], q, NT) * SCALE, masked_value)
    probs = jnp.exp(scores - row(atop + jnp.log(atotal)))
    va_acc[...] += dot(probs.astype(jnp.bfloat16), push)
    dp = dot(va_ref[0], push, NT)
    shift = jnp.sum(probs * dp, 0, keepdims=True)
    ka_acc[...] += dot((probs * (dp - shift)).astype(jnp.bfloat16), q)

    @pl.when(block == pl.num_programs(2) - 1)
    def _():
        for kind, value in ((0, ka_acc[...] * SCALE), (1, va_acc[...])):
            start = pl.multiple_of((kind * heads + head) * HEAD_SIZE, HEAD_SIZE)
            da_ref[0, :, pl.ds(start, HEAD_SIZE)] = value.astype(jnp.bfloat16)


def attention_specs(pieces, rows, heads, tile):
    def whole(shift):
        return pl.BlockSpec(
            (pieces, 1, rows, HEAD_SIZE), lambda s, h, b, *_: (0, s, 0, h + shift * heads)
        )

    stat = pl.BlockSpec((1, 1, tile), lambda s, h, b, *_: (s * heads + h, 0, b))
    keys = [whole(0), whole(1), whole(2)] + [whole(0), whole(1)] * 2
    return whole, stat, keys


def tile_pieces(pieces, rows):
    return min(pieces, max(1, 512 // rows))


def attend(me, offsets, triples, memory, older, added, reduced):
    pieces, count, rows, _ = triples.shape
    heads = memory.shape[-1] // (2 * HEAD_SIZE)
    padded, length = added.shape[1], pieces * rows
    many = tile_pieces(pieces, rows)
    whole, stat, keys = attention_specs(pieces, rows, heads, many * rows)
    for shift in (0, heads):
        keys.append(
            pl.BlockSpec((1, padded, HEAD_SIZE), lambda s, h, b, *_, shift=shift: (s, 0, h + shift))
        )
    tokens = jax.ShapeDtypeStruct((pieces, count, rows, heads * HEAD_SIZE), jnp.bfloat16)
    stats = jax.ShapeDtypeStruct((count * heads, 1, length), jnp.float32)
    work = count * heads * length * (3 * length + padded)
    return pl.pallas_call(
        functools.partial(attend_kernel, reduced, many),
        grid_spec=pltpu.PrefetchScalarGridSpec(
            num_scalar_prefetch=2,
            grid=(count, heads, pieces // many),
            in_specs=keys,
            out_specs=[
                whole(0),
                stat,
                pl.BlockSpec((1, *added.shape[1:]), lambda s, h, b, *_: (s, 0, 0)),
                pl.BlockSpec((8, HEAD_SIZE), lambda *_: (0, 0)),
            ],
            scratch_shapes=[pltpu.VMEM((padded, HEAD_SIZE), jnp.float32)] * 2,
        ),
        out_shape=[
            tokens,
            stats,
            jax.ShapeDtypeStruct(added.shape, jnp.bfloat16),
            jax.ShapeDtypeStruct((8, HEAD_SIZE), jnp.float32),
        ],
        cost_estimate=pl.CostEstimate(
            flops=work * 4 * HEAD_SIZE * 2, bytes_accessed=work // 64, transcendentals=work
        ),
        name="attend",
    )(me, offsets, triples, triples, triples, memory, memory, older, older, added, added)


def attend_back_kernel(
    many,
    heads,
    me_ref,
    offsets_ref,
    q_ref,
    kx_ref,
    vx_ref,
    km_ref,
    vm_ref,
    kc_ref,
    vc_ref,
    o_ref,
    do_ref,
    lse_ref,
    dx_ref,
    dm_ref,
    dc_ref,
    kx_acc,
    vx_acc,
    km_acc,
    vm_acc,
    kc_acc,
    vc_acc,
):
    seq, head, block = pl.program_id(0), pl.program_id(1), pl.program_id(2)
    pieces, _, rows, _ = q_ref.shape
    length, tile = pieces * rows, many * rows
    tiles = Tiles(me_ref[0], pieces, rows, many)
    offset = offsets_ref[seq]
    q, grad = tiles.load(q_ref, block, 0), tiles.load(do_ref, block, 0)

    @pl.when(block == 0)
    def _():
        for ref in (kx_acc, vx_acc, km_acc, vm_acc, kc_acc, vc_acc):
            ref[...] = jnp.zeros_like(ref)

    lse = lse_ref[0]
    both = grad.astype(jnp.float32) * tiles.load(o_ref, block, 0).astype(jnp.float32)
    delta = jnp.sum(jnp.transpose(both), 0, keepdims=True)

    def piece(keys, values, allowed):
        scores = dot(keys, q, NT) * SCALE
        if allowed is not None:
            scores = jnp.where(allowed, scores, masked_value)
        probs = jnp.exp(scores - lse)
        dv = dot(probs.astype(jnp.bfloat16), grad)
        dp = dot(values, grad, NT)
        ds = (probs * (dp - delta)).astype(jnp.bfloat16)
        return dot(ds, q), dv, dot(ds, keys, TN)

    dq = jnp.zeros((tile, HEAD_SIZE), jnp.float32)
    for base, keys_ref, values_ref, k_acc, v_acc in (
        (0, kc_ref, vc_ref, kc_acc, vc_acc),
        (length, km_ref, vm_ref, km_acc, vm_acc),
    ):
        for (first, keys), (_, values) in zip(tiles.chunks(keys_ref), tiles.chunks(values_ref)):
            dk, dv, part = piece(keys, values, tiles.place(first, 0) + base >= offset)
            k_acc[first : first + many] += dk.reshape(many, rows, HEAD_SIZE)
            v_acc[first : first + many] += dv.reshape(many, rows, HEAD_SIZE)
            dq += part

    def token_tile(index, allowed, dq):
        dk, dv, part = piece(tiles.load(kx_ref, index, 0), tiles.load(vx_ref, index, 0), allowed)
        tiles.store(kx_acc, index, dk, add=True)
        tiles.store(vx_acc, index, dv, add=True)
        return dq + part

    dq = lax.fori_loop(0, block, lambda index, dq: token_tile(index, None, dq), dq)
    causal = lax.broadcasted_iota(jnp.int32, (tile, tile), 0) <= lax.broadcasted_iota(
        jnp.int32, (tile, tile), 1
    )
    dq = token_tile(block, causal, dq)

    def columns(kind):
        return pl.ds(pl.multiple_of((kind * heads + head) * HEAD_SIZE, HEAD_SIZE), HEAD_SIZE)

    tiles.store(dx_ref, block, (dq * SCALE).astype(jnp.bfloat16), 0, slice(None), columns(0))

    @pl.when(block == pl.num_programs(2) - 1)
    def _():
        dx_ref[:, 0, :, columns(1)] = (kx_acc[...] * SCALE).astype(jnp.bfloat16)
        dx_ref[:, 0, :, columns(2)] = vx_acc[...].astype(jnp.bfloat16)
        dm_ref[:, 0, :, columns(0)] = (km_acc[...] * SCALE).astype(jnp.bfloat16)
        dm_ref[:, 0, :, columns(1)] = vm_acc[...].astype(jnp.bfloat16)
        dc_ref[:, 0, :, columns(0)] = (kc_acc[...] * SCALE).astype(jnp.bfloat16)
        dc_ref[:, 0, :, columns(1)] = vc_acc[...].astype(jnp.bfloat16)


def attend_back(me, offsets, triples, memory, older, out, grad, lse):
    pieces, count, rows, _ = triples.shape
    heads = memory.shape[-1] // (2 * HEAD_SIZE)
    length = pieces * rows
    many = tile_pieces(pieces, rows)
    whole, stat, keys = attention_specs(pieces, rows, heads, many * rows)

    def result(like):
        return pl.BlockSpec((pieces, 1, rows, like.shape[-1]), lambda s, h, b, *_: (0, s, 0, 0))

    outputs = [triples, memory, older]
    work = count * heads * length * 3 * length
    return pl.pallas_call(
        functools.partial(attend_back_kernel, many, heads),
        grid_spec=pltpu.PrefetchScalarGridSpec(
            num_scalar_prefetch=2,
            grid=(count, heads, pieces // many),
            in_specs=keys + [whole(0), whole(0), stat],
            out_specs=[result(like) for like in outputs],
            scratch_shapes=[pltpu.VMEM((pieces, rows, HEAD_SIZE), jnp.float32)] * 6,
        ),
        out_shape=[jax.ShapeDtypeStruct(like.shape, jnp.bfloat16) for like in outputs],
        cost_estimate=pl.CostEstimate(
            flops=work * 10 * HEAD_SIZE * 2, bytes_accessed=work // 32, transcendentals=work
        ),
        name="attend_back",
    )(
        me,
        offsets,
        triples,
        triples,
        triples,
        memory,
        memory,
        older,
        older,
        out,
        grad,
        lse,
    )


def feedforward_kernel(chunk, rows_ref, grad_ref, up_ref, down_ref, *refs):
    if len(refs) > 4:
        up_in, down_in, out_ref, back_ref, gup_ref, gdown_ref, up_acc, down_acc = refs
    else:
        out_ref, back_ref, up_acc, down_acc = refs
    width, hidden = up_ref.shape
    rows, grad = rows_ref[...].reshape(-1, width), grad_ref[...].reshape(-1, width)
    out = back = None

    @pl.when(pl.program_id(0) == 0)
    def _():
        if len(refs) > 4:
            up_acc[...] = up_in[...]
            down_acc[...] = down_in[...]
        else:
            up_acc[...] = jnp.zeros_like(up_acc)
            down_acc[...] = jnp.zeros_like(down_acc)

    for start in range(0, hidden, chunk):
        part = slice(start, start + chunk)
        up, down = up_ref[:, part], down_ref[part]
        u = dot(rows, up)
        root, cube = 0.7978845608028654, 0.044715
        square = u * u
        bend = jnp.tanh(root * (u + cube * (square * u)))
        half = 0.5 * (1.0 + bend)
        active = (u * half).astype(jnp.bfloat16)
        slope = half + 0.5 * u * (1.0 - bend * bend) * (root * (1.0 + 3.0 * cube * square))
        pre = (dot(grad, down, NT) * slope).astype(jnp.bfloat16)
        fresh = dot(active, down)
        out = fresh if out is None else out + fresh
        fresh = dot(pre, up, NT)
        back = fresh if back is None else back + fresh
        down_acc[part] += dot(active, grad, TN)
        up_acc[:, part] += dot(rows, pre, TN)
    out_ref[...] = out.astype(jnp.bfloat16).reshape(out_ref.shape)
    back_ref[...] = back.astype(jnp.bfloat16).reshape(back_ref.shape)
    if len(refs) > 4:

        @pl.when(pl.program_id(0) == pl.num_programs(0) - 1)
        def _():
            gup_ref[...] = up_acc[...].astype(gup_ref.dtype)
            gdown_ref[...] = down_acc[...].astype(gdown_ref.dtype)


def feedforward(rows, grad, up, down, before):
    pieces, count, each, width = rows.shape
    hidden = up.shape[1]
    many = min(pieces, max(1, 512 // (count * each)))
    block = pl.BlockSpec((many, count, each, width), lambda s: (s, 0, 0, 0))

    def whole(like):
        return pl.BlockSpec(like.shape, lambda s: (0, 0), pipeline_mode=pl.Buffered(1))

    kind = jnp.bfloat16 if before else jnp.float32
    total = pieces * count * each
    return pl.pallas_call(
        functools.partial(feedforward_kernel, min(512, hidden)),
        grid=(pieces // many,),
        in_specs=[block, block, whole(up), whole(down)] + [whole(up), whole(down)] * bool(before),
        out_specs=[block, block, whole(up), whole(down)],
        scratch_shapes=[
            pltpu.VMEM(up.shape, jnp.float32),
            pltpu.VMEM(down.shape, jnp.float32),
        ]
        * bool(before),
        out_shape=[jax.ShapeDtypeStruct(rows.shape, jnp.bfloat16)] * 2
        + [jax.ShapeDtypeStruct(up.shape, kind), jax.ShapeDtypeStruct(down.shape, kind)],
        cost_estimate=pl.CostEstimate(
            flops=12 * total * width * hidden,
            bytes_accessed=8 * total * width + 12 * width * hidden,
            transcendentals=total * hidden,
        ),
        name="feedforward",
    )(rows, grad, up, down, *before)


def stack_kernel(reduced, me_ref, memory_ref, stacked_ref, rows_acc):
    pieces, _, rows, width = memory_ref.shape
    blocks, extent, lanes = rows_acc.shape
    padded = stacked_ref.shape[1]
    keep = lax.broadcasted_iota(jnp.int32, (padded, 1), 0) < reduced
    for block in range(blocks):
        columns = slice(block * lanes, (block + 1) * lanes)
        for piece in range(pieces):
            start = pl.multiple_of((me_ref[0] ^ piece) * rows, rows)
            rows_acc[block, pl.ds(start, rows)] = memory_ref[piece, 0, :, columns].astype(
                jnp.float32
            )
        rows_acc[block, pieces * rows :] = jnp.zeros((extent - pieces * rows, lanes), jnp.float32)
        for tap in range(3):
            taken = rows_acc[block, pl.ds(tap, padded, stride=3)]
            start = tap * width + block * lanes
            stacked_ref[0, :, start : start + lanes] = jnp.where(keep, taken, 0.0).astype(
                jnp.bfloat16
            )


def stack(me, memory, reduced, padded):
    pieces, count, rows, width = memory.shape
    return pl.pallas_call(
        functools.partial(stack_kernel, reduced),
        grid_spec=pltpu.PrefetchScalarGridSpec(
            num_scalar_prefetch=1,
            grid=(count,),
            in_specs=[pl.BlockSpec((pieces, 1, rows, width), lambda s, *_: (0, s, 0, 0))],
            out_specs=pl.BlockSpec((1, padded, 3 * width), lambda s, *_: (s, 0, 0)),
            scratch_shapes=[pltpu.VMEM((width // 128, 3 * padded, 128), jnp.float32)],
        ),
        out_shape=jax.ShapeDtypeStruct((count, padded, 3 * width), jnp.bfloat16),
        cost_estimate=pl.CostEstimate(
            flops=0, bytes_accessed=4 * memory.size, transcendentals=0
        ),
        name="stack_memory",
    )(me, memory)


def fetch_kernel(dp, tensor, activations, weights, *refs):
    half, columns = tensor // 2, dp // 2
    count = len(activations) + len(weights)
    inputs, outputs = refs[:count], refs[count : 2 * count]
    staged, (send, recv, stage_sem) = refs[2 * count : -3], refs[-3:]
    place, plane = lax.axis_index("dp"), lax.axis_index("tensor")
    core, column = place % 2, place // 2
    upper, lower = plane // half, plane % half
    stays = core == upper

    def other(column, core, upper, lower):
        return (2 * column + core, upper * half + lower)

    swapped = other(column, upper, core, lower)
    row_bits = [1 << i for i in range(half.bit_length() - 1)] + [half]
    column_bits = [1 << i for i in range(columns.bit_length() - 1)]

    def row_partner(bit):
        if bit == half:
            return other(column, 1 - core, upper, lower)
        return other(column, core, upper, lower ^ bit)

    def column_partner(bit):
        return other(column ^ bit, core, upper, lower)

    partners = [row_partner(bit) for bit in row_bits] + [column_partner(b) for b in column_bits]

    loads = []
    for i in range(len(weights)):
        source = inputs[len(activations) + i]
        rows = staged[i].shape[0]
        load = pltpu.make_async_copy(
            source.at[pl.ds(pl.multiple_of(column * rows, rows), rows)], staged[i], stage_sem.at[i]
        )
        load.start()
        loads.append(load)

    barrier = pltpu.get_barrier_semaphore()
    for partner in partners:
        pl.semaphore_signal(barrier, 1, device_id=partner, device_id_type=pl.DeviceIdType.MESH)

    @pl.when(stays)
    def _():
        pl.semaphore_wait(barrier, len(partners))

    @pl.when(jnp.logical_not(stays))
    def _():
        pl.semaphore_signal(barrier, 1, device_id=swapped, device_id_type=pl.DeviceIdType.MESH)
        pl.semaphore_wait(barrier, len(partners) + 1)

    for load in loads:
        load.wait()

    transfers = []
    for item in range(count):
        if item < len(activations):
            source, where, bits, partner = inputs[item], 0, row_bits, row_partner
        else:
            source, where = staged[item - len(activations)], column
            bits, partner = column_bits, column_partner
        transfers.append((item, source, where, bits, partner))
    ranks = activations + weights
    order = sorted(range(count), key=lambda item: ranks[item])

    def keep(item):
        _, source, where, _, _ = transfers[item]
        return pltpu.make_async_copy(source, outputs[item].at[where], recv.at[item, 0])

    def swap(item):
        _, source, where, _, _ = transfers[item]
        return pltpu.make_async_remote_copy(
            source,
            outputs[item].at[where],
            send.at[item, 0],
            recv.at[item, 0],
            device_id=swapped,
            device_id_type=pl.DeviceIdType.MESH,
        )

    def exchange(item, stage):
        _, _, where, bits, partner = transfers[item]
        bit = bits[stage - 1]
        if item < len(activations):
            source, target = outputs[item].at[pl.ds(0, bit)], outputs[item].at[pl.ds(bit, bit)]
        else:
            block = pl.ds(column // bit * bit, bit)
            source = target = outputs[item].at[block]
        return pltpu.make_async_remote_copy(
            source,
            target,
            send.at[item, stage],
            recv.at[item, stage],
            device_id=partner(bit),
            device_id_type=pl.DeviceIdType.MESH,
        )

    def begin(item):
        @pl.when(stays)
        def _():
            keep(item).start()

        @pl.when(jnp.logical_not(stays))
        def _():
            swap(item).start()

    ahead = 2
    for item in order[:ahead]:
        begin(item)

    depth = max(len(row_bits), len(column_bits))
    for tick in range(len(order) + depth):
        if tick + ahead < len(order):
            begin(order[tick + ahead])
        for stage in range(1, depth + 2):
            index = tick - stage + 1
            if not 0 <= index < len(order):
                continue
            item = order[index]
            bits = transfers[item][3]
            if stage == 1:

                @pl.when(stays)
                def _(item=item):
                    keep(item).wait()

                @pl.when(jnp.logical_not(stays))
                def _(item=item):
                    swap(item).wait_recv()

            elif stage <= len(bits) + 1:
                exchange(item, stage - 1).wait_recv()
            if stage <= len(bits):
                exchange(item, stage).start()

    @pl.when(jnp.logical_not(stays))
    def _():
        for item in order:
            swap(item).wait_send()

    for item in order:
        for stage in range(1, len(transfers[item][3]) + 1):
            exchange(item, stage).wait_send()


def fetch(layout, activations, weights):
    columns, tensor = layout.columns, layout.tensor
    arrays = [value for _, value in activations + weights]
    slices = [(value.shape[0] // columns, *value.shape[1:]) for _, value in weights]
    shapes = [(tensor, *value.shape) for _, value in activations] + [
        (columns, *part) for part in slices
    ]
    stages = tensor.bit_length() + columns.bit_length()
    results = pl.pallas_call(
        functools.partial(
            fetch_kernel,
            layout.dp,
            tensor,
            [rank for rank, _ in activations],
            [rank for rank, _ in weights],
        ),
        in_specs=[pl.BlockSpec(memory_space=pltpu.VMEM)] * len(activations)
        + [pl.BlockSpec(memory_space=pl.ANY)] * len(weights),
        out_specs=[pl.BlockSpec(memory_space=pl.ANY)] * len(arrays),
        out_shape=[jax.ShapeDtypeStruct(shape, jnp.bfloat16) for shape in shapes],
        scratch_shapes=[pltpu.VMEM(part, jnp.bfloat16) for part in slices]
        + [
            pltpu.SemaphoreType.DMA((len(arrays), stages)),
            pltpu.SemaphoreType.DMA((len(arrays), stages)),
            pltpu.SemaphoreType.DMA((len(weights),)),
        ],
        compiler_params=pltpu.CompilerParams(collective_id=0, has_side_effects=True),
        name="fetch",
    )(*arrays)
    whole = results[len(activations) :]
    return results[: len(activations)], [
        part.reshape(value.shape) for part, (_, value) in zip(whole, weights)
    ]


class Links:
    def __init__(self, dp, tensor, send, recv):
        self.half, self.columns = tensor // 2, dp // 2
        self.send, self.recv, self.used, self.sent = send, recv, 0, []
        place, plane = lax.axis_index("dp"), lax.axis_index("tensor")
        self.core, self.column = place % 2, place // 2
        self.upper, self.lower = plane // self.half, plane % self.half
        self.stays = self.core == self.upper
        self.row_bits = [1 << i for i in range(self.half.bit_length() - 1)] + [self.half]
        self.column_bits = [1 << i for i in range(self.columns.bit_length() - 1)]

    def at(self, column=None, core=None, upper=None, lower=None):
        column = self.column if column is None else column
        core = self.core if core is None else core
        upper = self.upper if upper is None else upper
        lower = self.lower if lower is None else lower
        return (2 * column + core, upper * self.half + lower)

    def row(self, bit):
        if bit == self.half:
            return self.at(core=1 - self.core)
        return self.at(lower=self.lower ^ bit)

    def swapped(self):
        return self.at(core=self.upper, upper=self.core)

    def greet(self):
        partners = [self.row(bit) for bit in self.row_bits]
        partners += [self.at(column=self.column ^ bit) for bit in self.column_bits]
        partners.append(self.at(upper=1 - self.upper))
        barrier = pltpu.get_barrier_semaphore()

        def signal(partner):
            pl.semaphore_signal(barrier, 1, device_id=partner, device_id_type=pl.DeviceIdType.MESH)

        for partner in partners:
            signal(partner)

        @pl.when(self.stays)
        def _():
            pl.semaphore_wait(barrier, len(partners))

        @pl.when(jnp.logical_not(self.stays))
        def _():
            signal(self.swapped())
            pl.semaphore_wait(barrier, len(partners) + 1)

    def slot(self):
        self.used += 1
        return self.used - 1

    def copy(self, source, target, partner, slot=None):
        slot = self.slot() if slot is None else slot
        return pltpu.make_async_remote_copy(
            source,
            target,
            self.send.at[slot],
            self.recv.at[slot],
            device_id=partner,
            device_id_type=pl.DeviceIdType.MESH,
        )

    def put(self, source, target, partner):
        copy = self.copy(source, target, partner)
        copy.start()
        self.sent.append(copy)
        return copy

    def finish(self):
        for copy in self.sent:
            copy.wait_send()


def reduce_rows(links, partial, received, work, result):
    arrived = []
    for step, bit in enumerate(reversed(links.row_bits)):
        source = partial
        if step:
            source = work
            for piece in range(bit, 2 * bit):
                value = partial[piece].astype(jnp.float32)
                for other in arrived:
                    value += other[piece].astype(jnp.float32)
                work[piece] = value.astype(jnp.bfloat16)
        copy = links.put(source.at[pl.ds(bit, bit)], received[step], links.row(bit))
        yield
        copy.wait_recv()
        arrived.append(received[step])
    value = partial[0].astype(jnp.float32)
    for other in arrived:
        value += other[0].astype(jnp.float32)
    result.append(value)


def gather_rows(links, whole):
    for bit in links.row_bits:
        copy = links.put(whole.at[pl.ds(0, bit)], whole.at[pl.ds(bit, bit)], links.row(bit))
        yield
        copy.wait_recv()


def return_rows(links, value, mine, target):
    copy = links.copy(mine, target, links.swapped())

    @pl.when(links.stays)
    def _():
        target[...] = value

    @pl.when(jnp.logical_not(links.stays))
    def _():
        mine[...] = value
        copy.start()

    yield

    @pl.when(jnp.logical_not(links.stays))
    def _():
        copy.wait_recv()
        copy.wait_send()


def reduce_columns(links, bits, grad, received, work, quarter, across, store):
    left = list(bits)
    arrived = []

    def relative(some):
        found = [0]
        for bit in some:
            found += [value | bit for value in found]
        return found

    def value_of(place):
        value = grad[links.column ^ place].astype(jnp.float32)
        for other, slots in arrived:
            value += other[slots.index(place)].astype(jnp.float32)
        return value

    for step, bit in enumerate(bits):
        left.remove(bit)
        slots = relative(left)
        copies = []
        for slot, place in enumerate(slots):
            if step:
                work[slot] = value_of(place | bit).astype(jnp.bfloat16)
                source = work.at[slot]
            else:
                source = grad.at[links.column ^ (place | bit)]
            copies.append(
                links.put(
                    source, received[step].at[slot], links.at(column=links.column ^ bit)
                )
            )
        yield
        for copy in copies:
            copy.wait_recv()
        arrived.append((received[step], slots))
    value = value_of(0)
    rows = value.shape[0] // 2
    quarter[0] = value[:rows].astype(jnp.bfloat16)
    quarter[1] = value[rows:].astype(jnp.bfloat16)
    first, slot = quarter.at[1 - links.upper], links.slot()
    to_core = links.copy(first, across.at[0], links.at(core=1 - links.core), slot)
    to_half = links.copy(first, across.at[0], links.at(upper=1 - links.upper), slot)
    to_swapped = links.copy(quarter.at[links.upper], across.at[1], links.swapped())

    @pl.when(links.stays)
    def _():
        to_core.start()

    @pl.when(jnp.logical_not(links.stays))
    def _():
        to_half.start()
        to_swapped.start()

    yield
    to_core.wait()

    @pl.when(links.stays)
    def _():
        total = quarter[links.upper].astype(jnp.float32) + across[0].astype(jnp.float32)
        store(total.astype(jnp.bfloat16))

    @pl.when(jnp.logical_not(links.stays))
    def _():
        to_swapped.wait()
        total = across[1].astype(jnp.float32) + across[0].astype(jnp.float32)
        store(total.astype(jnp.bfloat16))


def gather_columns(links, bits, result):
    places = [0]
    for bit in bits:
        copies = []
        for place in places:
            part = result.at[links.column ^ place, links.core]
            copies.append(links.put(part, part, links.at(column=links.column ^ bit)))
        yield
        for copy in copies:
            copy.wait_recv()
        places += [place | bit for place in places]
    part = result.at[:, links.core]
    copy = links.put(part, part, links.at(core=1 - links.core))
    yield
    copy.wait_recv()


def sum_all(links, source, slots, result):
    value = source[...]
    partners = [links.row(bit) for bit in links.row_bits] + [links.at(upper=1 - links.upper)]
    partners += [links.at(column=links.column ^ bit) for bit in links.column_bits]
    for step, partner in enumerate(partners):
        slots[2 * step] = value
        copy = links.put(slots.at[2 * step], slots.at[2 * step + 1], partner)
        yield
        copy.wait_recv()
        value = value + slots[2 * step + 1]
    result[...] = value


def run_streams(links, streams, order):
    alive = dict(enumerate(streams))

    def advance(index):
        if index in alive:
            try:
                next(alive[index])
            except StopIteration:
                del alive[index]

    for index in order:
        advance(index)
    while alive:
        for index in list(alive):
            advance(index)
    links.finish()


def row_buffers(shape):
    pieces, *rest = shape
    sizes, bit = [], pieces // 2
    while bit:
        sizes.append(bit)
        bit //= 2
    return [pltpu.VMEM((size, *rest), jnp.bfloat16) for size in sizes + [pieces // 2]]


def column_buffers(shape):
    columns, rows, width = shape
    sizes, count = [], columns // 2
    while count:
        sizes.append(count)
        count //= 2
    return [pltpu.VMEM((size, rows, width), jnp.bfloat16) for size in sizes] + [
        pltpu.VMEM((max(1, columns // 4), rows, width), jnp.bfloat16),
        pltpu.VMEM((2, rows // 2, width), jnp.bfloat16),
        pltpu.VMEM((2, rows // 2, width), jnp.bfloat16),
    ]


def take(refs, count):
    taken = refs[:count]
    del refs[:count]
    return taken


def exchange(kernel, layout, collective_id, inputs, outputs, scratch, copies, name):
    vmem = pl.BlockSpec(memory_space=pltpu.VMEM)
    return pl.pallas_call(
        functools.partial(kernel, layout.dp, layout.tensor),
        in_specs=[vmem] * len(inputs),
        out_specs=[vmem] * len(outputs),
        out_shape=[jax.ShapeDtypeStruct(*each) for each in outputs],
        scratch_shapes=scratch
        + [pltpu.SemaphoreType.DMA((copies,)), pltpu.SemaphoreType.DMA((copies,))],
        compiler_params=pltpu.CompilerParams(collective_id=collective_id, has_side_effects=True),
        name=name,
    )(*inputs)


def middle_kernel(dp, tensor, *refs):
    refs = list(refs)
    links = Links(dp, tensor, *refs[-2:])
    gain = refs.pop(0)
    groups = [take(refs, 3) for _ in range(2)]
    outputs = [take(refs, 3) for _ in range(2)]
    count = len(links.row_bits) + 1
    buffers = [take(refs, 2 * count) for _ in range(2)]
    links.greet()

    def stream(inputs, results, spare):
        (partial, raw, _), (hidden, whole, _) = inputs, results
        found = []
        yield from reduce_rows(links, partial, spare[: count - 1], spare[count - 1], found)
        value = raw[...].astype(jnp.float32) + found[0]
        hidden[...] = value
        whole[0] = (normalize(value)[0] * gain[...]).astype(jnp.bfloat16)
        yield from gather_rows(links, whole)

    def appended(inputs, results, spare):
        found = []
        yield from reduce_rows(links, inputs[2], spare[count:-1], spare[-1], found)
        results[2][...] = found[0].astype(jnp.bfloat16)

    each = list(zip(groups, outputs, buffers))
    streams = [stream(*one) for one in each] + [appended(*one) for one in each]
    run_streams(links, streams, [0, 1, 2, 3, 0, 1, 0, 2, 3, 1, 0, 1])


def middle(layout, gain, partials, raws, pieces):
    inputs = [gain.reshape(1, -1)]
    outputs, scratch = [], []
    for partial, raw, piece in zip(partials, raws, pieces):
        inputs += [partial, raw, piece]
        outputs += [
            (raw.shape, jnp.float32),
            (partial.shape, jnp.bfloat16),
            (piece.shape[1:], jnp.bfloat16),
        ]
        scratch += row_buffers(partial.shape) + row_buffers(piece.shape)
    copies = 6 * layout.tensor.bit_length()
    return exchange(middle_kernel, layout, 1, inputs, outputs, scratch, copies, "middle")


def middle_back_kernel(dp, tensor, *refs):
    refs = list(refs)
    links = Links(dp, tensor, *refs[-2:])
    gain = refs.pop(0)
    groups = [take(refs, 3) for _ in range(2)]
    grads = take(refs, 3)
    gain_sum = refs.pop(0)
    outputs = [take(refs, 2) for _ in range(2)]
    results = take(refs, 3)
    buffers = [take(refs, len(links.row_bits) + 1) for _ in range(2)]
    spares = [take(refs, len(links.column_bits) + 3) for _ in range(3)]
    links.greet()
    gain_sum[...] = jnp.zeros_like(gain_sum)

    def stream(inputs, results, spare):
        (partial, hidden, cotangent), (grad_hidden, whole) = inputs, results
        found = []
        yield from reduce_rows(links, partial, spare[:-1], spare[-1], found)
        unit, inverse = normalize(hidden[...])
        width = unit.shape[-1]
        gain_sum[...] += jnp.sum((found[0] * unit).reshape(-1, 8, width), 0)
        value = cotangent[...].astype(jnp.float32) + norm_back(
            found[0], gain[...], unit, inverse
        )
        grad_hidden[...] = value
        whole[0] = value.astype(jnp.bfloat16)
        yield from gather_rows(links, whole)

    def column(bits, grad, result, spare):
        def store(value):
            result[...] = value

        yield from reduce_columns(links, bits, grad, spare[:-3], *spare[-3:], store)

    bits = links.column_bits
    streams = [stream(*each) for each in zip(groups, outputs, buffers)] + [
        column(order, *each)
        for order, each in zip((bits, bits[::-1], bits), zip(grads, results, spares))
    ]
    run_streams(links, streams, [0, 1, 4, 2, 3, 0, 1, 0, 4, 1, 2, 3, 4, 2, 3, 0, 1])


def middle_back(layout, gain, partials, hiddens, cotangents, grads):
    inputs = [gain.reshape(1, -1)]
    outputs, scratch = [((8, gain.shape[0]), jnp.float32)], []
    for partial, hidden, cotangent in zip(partials, hiddens, cotangents):
        inputs += [partial, hidden, cotangent]
        outputs += [(hidden.shape, jnp.float32), (partial.shape, jnp.bfloat16)]
        scratch += row_buffers(partial.shape)
    for grad in grads:
        split = layout.split(grad)
        inputs.append(split)
        outputs.append((layout.eighths(grad)[2:], jnp.bfloat16))
        scratch += column_buffers(split.shape)
    copies = 4 * layout.tensor.bit_length() + 3 * (layout.columns + 4)
    return exchange(middle_back_kernel, layout, 2, inputs, outputs, scratch, copies, "middle_back")


def leave_kernel(dp, tensor, *refs):
    refs = list(refs)
    links = Links(dp, tensor, *refs[-2:])
    gain, sums = take(refs, 2)
    tokens = [take(refs, 3) for _ in range(2)]
    outs = [take(refs, 2) for _ in range(2)]
    grads = take(refs, 2)
    total = refs.pop(0)
    targets, results = take(refs, 4), take(refs, 2)
    slots = refs.pop(0)
    buffers = [take(refs, len(links.row_bits) + 2) for _ in range(4)]
    spares = [take(refs, len(links.column_bits) + 3) for _ in range(2)]
    links.greet()

    def token_stream(inputs, target, spare):
        partial, raw, grad_hidden = inputs
        found = []
        yield from reduce_rows(links, partial, spare[:-2], spare[-2], found)
        unit, inverse = normalize(raw[...].astype(jnp.float32))
        value = grad_hidden[...] + norm_back(found[0], gain[...], unit, inverse)
        yield from return_rows(links, value.astype(jnp.bfloat16), spare[-1], target)

    def out_stream(inputs, target, spare):
        partial, hidden = inputs
        found = []
        yield from reduce_rows(links, partial, spare[:-2], spare[-2], found)
        value = (hidden[...] + found[0]).astype(jnp.bfloat16)
        yield from return_rows(links, value, spare[-1], target)

    def column(bits, grad, result, spare):
        def store(value):
            result[links.column, links.core] = value

        yield from reduce_columns(links, bits, grad, spare[:-3], *spare[-3:], store)
        yield from gather_columns(links, bits, result)

    bits = links.column_bits
    streams = [token_stream(*each) for each in zip(tokens, targets[:2], buffers[:2])]
    streams += [out_stream(*each) for each in zip(outs, targets[2:], buffers[2:])]
    streams += [column(*each) for each in zip((bits, bits[::-1]), grads, results, spares)]
    streams.append(sum_all(links, sums, slots, total))
    order = [0, 1, 4, 5, 2, 3, 6, 0, 1, 6, 5, 0, 2, 6, 4, 5, 1, 4, 5, 3, 6, 2, 4, 5, 6, 4, 5, 3]
    run_streams(links, streams, order)


def leave(layout, gain, sums, tokens, outs, grads):
    inputs = [gain.reshape(1, -1), sums]
    steps = (layout.dp * layout.tensor).bit_length() - 1
    outputs, scratch = [(sums.shape, jnp.float32)], [
        pltpu.VMEM((2 * steps, *sums.shape), jnp.float32)
    ]
    for each in tokens + outs:
        inputs += each
        owned = each[1].shape
        outputs.append((owned, jnp.bfloat16))
        scratch += row_buffers(each[0].shape) + [pltpu.VMEM(owned, jnp.bfloat16)]
    for grad in grads:
        inputs.append(layout.split(grad))
        outputs.append((layout.eighths(grad), jnp.bfloat16))
        scratch += column_buffers(inputs[-1].shape)
    copies = 4 * (layout.tensor.bit_length() + 1) + steps + 4 * (layout.columns + 4)
    return exchange(leave_kernel, layout, 3, inputs, outputs, scratch, copies, "leave")


class Group:
    def __init__(self, layout, tokens, memory, older, cotangent, offsets):
        self.layout, self.offsets = layout, layout.swap(offsets)
        self.me = layout.shard.reshape(1).astype(jnp.int32)
        self.count = tokens.shape[1]
        self.length = tokens.shape[2] * layout.tensor
        self.reduced = self.length // 3
        self.padded = -(-self.reduced // 128) * 128
        self.token_rows, self.memory_rows, self.older_rows = tokens, memory, older
        self.grad_rows = cotangent
        self.raw, self.cotangent = tokens[0], cotangent[0]

    def enter(self, gain):
        self.token_z = normed(self.token_rows, gain)
        self.memory_z = normed(self.memory_rows, gain)
        self.older_z = normed(self.older_rows, gain)
        self.stacked = stack(self.me, self.memory_rows, self.reduced, self.padded)

    def compress(self, squeeze, pair_weight, gain):
        layout = self.layout
        self.appended = matmul(self.stacked, squeeze).astype(jnp.bfloat16)
        whole = layout.ordered(layout.gather(self.appended), -1)
        self.added_unit, self.added_inverse = normalize(whole.astype(jnp.float32))
        rows = (self.added_unit * gain).astype(jnp.bfloat16)
        self.added = matmul(rows, pair_weight).astype(jnp.bfloat16)

    def attend(self, triple_weight, pair_weight):
        self.triples = matmul(self.token_z, triple_weight).astype(jnp.bfloat16)
        self.memory_pairs = matmul(self.memory_z, pair_weight).astype(jnp.bfloat16)
        self.older_pairs = matmul(self.older_z, pair_weight).astype(jnp.bfloat16)
        self.attention, self.lse, self.grad_added, squares = attend(
            self.me,
            self.offsets,
            self.triples,
            self.memory_pairs,
            self.older_pairs,
            self.added,
            self.reduced,
        )
        self.squares = jnp.sum(squares)

    def feed(self, up_weight, down_weight, before):
        self.feed_out, self.feed_back, grad_up, grad_down = feedforward(
            self.feed_rows, self.grad_rows, up_weight, down_weight, before
        )
        return grad_up, grad_down

    def branch_back(self, whole, out_weight):
        self.grad_attention = matmul_back(whole, out_weight).astype(jnp.bfloat16)
        return outer(self.attention, whole)

    def attend_back(self):
        self.grad_triples, self.grad_memory, self.grad_older = attend_back(
            self.me,
            self.offsets,
            self.triples,
            self.memory_pairs,
            self.older_pairs,
            self.attention,
            self.grad_attention,
            self.lse,
        )

    def compress_back(self, pair_weight, gain):
        layout = self.layout
        grad = matmul_back(self.grad_added, pair_weight)
        grad = norm_back(grad, gain, self.added_unit, self.added_inverse).astype(jnp.bfloat16)
        extent = self.appended.shape[2]
        return jnp.stack(
            [
                lax.dynamic_slice_in_dim(grad, (layout.shard ^ j) * extent, extent, 2)
                for j in range(layout.tensor)
            ]
        )


    def projection_grads(self):
        width = self.grad_triples.shape[-1] // 3
        triple = outer(self.token_z, self.grad_triples)
        pair = outer(self.memory_z, self.grad_memory) + outer(self.older_z, self.grad_older)
        return triple + jnp.pad(pair, ((0, 0), (width, 0)))

    def leave_appended(self):
        return self.layout.swap(self.appended)[:, : self.reduced]


def per_device(
    inputs_short,
    memory_short,
    compressed_short,
    offsets_short,
    inputs_long,
    memory_long,
    compressed_long,
    offsets_long,
    query_weight,
    key_weight,
    value_weight,
    out_weight,
    up_weight,
    down_weight,
    compress_weight,
    attention_gain,
    feedforward_gain,
    cotangent_short,
    cotangent_long,
):
    layout = Layout()
    width, local_width = query_weight.shape
    rows, whole = fetch(
        layout,
        [
            (0, inputs_short),
            (1, memory_short),
            (2, compressed_short),
            (8, cotangent_short),
            (3, inputs_long),
            (4, memory_long),
            (5, compressed_long),
            (9, cotangent_long),
        ],
        [
            (1.1, query_weight),
            (1.2, key_weight),
            (1.3, value_weight),
            (2.1, compress_weight.reshape(3 * width, local_width)),
            (3.1, out_weight),
            (4.1, up_weight),
            (5.1, down_weight),
        ],
    )
    triple_weight = jnp.concatenate(whole[:3], 1)
    pair_weight = triple_weight[:, local_width:]
    squeeze, output_weight, up, down = whole[3:]
    short = Group(layout, *rows[:4], offsets_short)
    long = Group(layout, *rows[4:], offsets_long)
    groups = (short, long)

    grad_out = grad_squeeze = grad_triple = 0.0
    pieces = []
    for group in groups[::-1]:
        group.enter(attention_gain)
        group.compress(squeeze, pair_weight, attention_gain)
        group.attend(triple_weight, pair_weight)
        pieces.append(group.compress_back(pair_weight, attention_gain))
    long.hidden, long.feed_rows, long_added, short.hidden, short.feed_rows, short_added = middle(
        layout,
        feedforward_gain,
        [matmul(group.attention, output_weight).astype(jnp.bfloat16) for group in (long, short)],
        [long.raw, short.raw],
        pieces,
    )
    grad_squeeze = outer(long.stacked, long_added) + outer(short.stacked, short_added)
    before = ()
    for group in groups:
        before = group.feed(up, down, before)
    feed_gain, long.grad_hidden, long_back, short.grad_hidden, short_back, *early = middle_back(
        layout,
        feedforward_gain,
        [long.feed_back, short.feed_back],
        [long.hidden, short.hidden],
        [long.cotangent, short.cotangent],
        [*before, grad_squeeze],
    )
    up_sum, down_sum, squeeze_sum = (
        lax.all_gather(eighth, "dp", axis=0, tiled=True).astype(jnp.float32) for eighth in early
    )
    for group, whole in ((long, long_back), (short, short_back)):
        grad_out += group.branch_back(whole, output_weight)
        group.attend_back()
        grad_triple += group.projection_grads()
    attention_part = (
        jnp.sum(grad_triple * triple_weight.astype(jnp.float32), 1) / attention_gain
    )
    sums = jnp.concatenate(
        [
            attention_part,
            jnp.sum(feed_gain, 0),
            jnp.full((1024,), short.squares + long.squares),
        ]
    ).reshape(-1, 128)
    sums, short_grad, long_grad, short_out, long_out, triple_sum, out_sum = leave(
        layout,
        attention_gain,
        sums,
        [
            [
                matmul_back(group.grad_triples, triple_weight).astype(jnp.bfloat16),
                group.raw,
                group.grad_hidden,
            ]
            for group in groups
        ],
        [[group.feed_out, group.hidden] for group in groups],
        [grad_triple, grad_out],
    )
    sums = sums.reshape(-1)
    triple_sum = triple_sum.reshape(triple_weight.shape).astype(jnp.float32)
    out_sum = out_sum.reshape(out_weight.shape).astype(jnp.float32)
    squeeze_sum = squeeze_sum.reshape(compress_weight.shape)
    gain_one, gain_two, square_total = sums[:width], sums[width : 2 * width], sums[2 * width]
    rows_all = sum(group.count * group.length for group in groups) * layout.dp
    return (
        short_out,
        long_out,
        short_grad.astype(jnp.float32),
        long_grad.astype(jnp.float32),
        short.leave_appended(),
        long.leave_appended(),
        triple_sum[:, :local_width],
        triple_sum[:, local_width : 2 * local_width],
        triple_sum[:, 2 * local_width :],
        out_sum,
        up_sum,
        down_sum,
        squeeze_sum,
        gain_one,
        gain_two,
        square_total / rows_all,
    )


def solution(mesh):
    in_specs = (
        P("dp", "tensor", None),
        P("dp", "tensor", None),
        P("dp", "tensor", None),
        P("dp"),
        P("dp", "tensor", None),
        P("dp", "tensor", None),
        P("dp", "tensor", None),
        P("dp"),
        P(None, "tensor"),
        P(None, "tensor"),
        P(None, "tensor"),
        P("tensor", None),
        P(None, "tensor"),
        P("tensor", None),
        P(None, None, "tensor"),
        P(),
        P(),
        P("dp", "tensor", None),
        P("dp", "tensor", None),
    )
    out_specs = (
        P("dp", "tensor", None),
        P("dp", "tensor", None),
        P("dp", "tensor", None),
        P("dp", "tensor", None),
        P("dp", None, "tensor"),
        P("dp", None, "tensor"),
        P(None, "tensor"),
        P(None, "tensor"),
        P(None, "tensor"),
        P("tensor", None),
        P(None, "tensor"),
        P("tensor", None),
        P(None, None, "tensor"),
        P(),
        P(),
        P(),
    )
    return jax.shard_map(
        per_device, mesh=mesh, in_specs=in_specs, out_specs=out_specs, check_vma=False
    )
```
